32 devices in a mesh: ex: 8 (over z, core), ey: 4 (over y, x).
Axes of the slice: x: 2, y: 2, z: 4, core: 2. Of those that a mesh axis runs over, the one named last changes fastest.
Arguments:
- right_side: float32 [48, 32, 1920], P('ex', 'ey'), may hold values from -300 to 300
- start_field: float32 [48, 32, 1920], P('ex', 'ey'), may hold values from -3 to 3
- coupling: float32 [5, 48, 32], P(None, 'ex', 'ey'), may hold values from 0.1 to 1.4
- mode_blocks: float32 [5, 120, 120], replicated, may hold values from -0.5 to 3
Outputs:
- updated_field: float32 [48, 32, 1920], P('ex', 'ey')
- new_residual: float32 [48, 32, 1920], P('ex', 'ey')
The draws below stay inside these ranges and needn't reach their ends.
All inputs are finite; a program needn't handle non-finite values.
Results may differ from the reference program's by a relative error of at most 0.017.
Values sent between devices are 32-bit elements; how exact they have to be, the bound alone decides.
A program may use at most 64 MiB of HBM per device.

```python
import math
import jax
import jax.numpy as jnp
from jax import lax

M = 120
R = 16
S = 4
GX = 6
GY = 8
NX = 48
NY = 32


def draw_right_side(key, part):
    first_key, second_key = jax.random.split(key, 2)
    row_pos = jnp.arange(NX, dtype=jnp.float32)[:, None] / NX
    col_pos = jnp.arange(NY, dtype=jnp.float32)[None, :] / NY
    rough = jax.random.uniform(second_key, (NX, NY), jnp.float32, 0.0, math.log(3.0))
    base = jnp.clip(jax.random.normal(first_key, (NX, NY, R * M), jnp.float32), -5.0, 5.0)
    scales = jnp.exp(math.log(3.0) * (row_pos + col_pos) + rough)
    return (base * scales[:, :, None]).astype(jnp.float32)


def draw_coupling(key, part):
    volume_key, face_key, block_key = jax.random.split(jax.random.fold_in(key, 11), 3)
    row_pos = jnp.arange(NX, dtype=jnp.float32)[:, None] / NX
    block_log = jax.random.uniform(block_key, (NX // GX, NY // GY), jnp.float32, 0.0, math.log(2.0))
    block_log = jnp.repeat(jnp.repeat(block_log, GX, axis=0, total_repeat_length=NX), GY, axis=1, total_repeat_length=NY)
    element_log = jax.random.uniform(volume_key, (NX, NY), jnp.float32, 0.0, math.log(1.1))
    volume = jnp.exp(math.log(0.3) + math.log(2.0) * row_pos + block_log + element_log)[None, :, :]
    faces = jnp.exp(jax.random.uniform(face_key, (4, NX, NY), jnp.float32, math.log(0.1), math.log(0.6)))
    return jnp.concatenate([volume, faces], axis=0).astype(jnp.float32)


def draw_mode_blocks(key, part):
    diag_key, noise_key = jax.random.split(jax.random.fold_in(key, 23), 2)
    noise = jnp.clip(jax.random.normal(noise_key, (5, M, M), jnp.float32), -4.0, 4.0) * (0.5 / math.sqrt(M))
    diag_values = jax.random.uniform(diag_key, (M,), jnp.float32, 1.5, 2.5)
    rows = jnp.arange(M)[:, None]
    cols = jnp.arange(M)[None, :]
    diag_matrix = jnp.where(rows == cols, diag_values[None, :], jnp.float32(0.0))
    volume_marker = (jnp.arange(5) == 0).astype(jnp.float32)[:, None, None]
    return (noise + volume_marker * diag_matrix[None, :, :]).astype(jnp.float32)


def block_levels(rng, shape, pieces, least, high):
    level, own = 1.0, jax.random.fold_in(rng, 6)
    for dim, parts in pieces:
        heights = jnp.exp(jax.random.uniform(jax.random.fold_in(own, dim), (parts,), jnp.float32, least / len(pieces), high / len(pieces)))
        level = level * jnp.repeat(heights, shape[dim] // parts).reshape([-1 if axis == dim else 1 for axis in range(len(shape))])
    return level


def scatter_about(own_key, extent, deviation, reach, cuts=(), kind=jnp.bfloat16):
    values = jax.random.normal(own_key, extent, jnp.float32) * deviation
    if len(cuts) > 0:
        values = block_levels(own_key, extent, cuts, -0.22, 0.18) * values
    return jnp.clip(values, min=-reach, max=reach).astype(kind)


def setup_inputs(seed: int = 0) -> dict:
    arg_keys = jax.random.split(jax.random.key(seed), 5)
    return {
        "right_side": draw_right_side(jax.random.fold_in(arg_keys[4], 71), 0),
        "start_field": scatter_about(arg_keys[1], (NX, NY, R * M), 0.5, 3.0, ((0, 8), (1, 4)), jnp.float32),
        "coupling": draw_coupling(jax.random.fold_in(arg_keys[4], 71), 0),
        "mode_blocks": draw_mode_blocks(jax.random.fold_in(arg_keys[4], 71), 0),
    }


highest = lax.Precision.HIGHEST

def on_modes(field_in, matrix):
    flattened = field_in.reshape(-1, matrix.shape[0])
    return jnp.dot(flattened.astype(jnp.float32), matrix.astype(jnp.float32), precision=highest, preferred_element_type=jnp.float32).reshape(field_in.shape)

def apply_operator(field_in, coupling, mode_blocks):
    padded = jnp.pad(field_in, ((1, 1), (1, 1), (0, 0)))
    result = coupling[0][:, :, None] * on_modes(field_in, mode_blocks[0])
    result = result + coupling[1][:, :, None] * on_modes(padded[:-2, 1:-1], mode_blocks[1])
    result = result + coupling[2][:, :, None] * on_modes(padded[2:, 1:-1], mode_blocks[2])
    result = result + coupling[3][:, :, None] * on_modes(padded[1:-1, :-2], mode_blocks[3])
    result = result + coupling[4][:, :, None] * on_modes(padded[1:-1, 2:], mode_blocks[4])
    return result

def gram_block(left_block, right_block):
    left_four = left_block.reshape(left_block.shape[0], left_block.shape[1], R, M)
    right_four = right_block.reshape(right_block.shape[0], right_block.shape[1], R, M)
    return jnp.einsum('ijrm,ijsm->rs', left_four.astype(jnp.float32), right_four.astype(jnp.float32), precision=highest, preferred_element_type=jnp.float32)

def combine_blocks(field_in, weights):
    four = field_in.reshape(field_in.shape[0], field_in.shape[1], R, M)
    mixed = jnp.einsum('ijrm,rs->ijsm', four.astype(jnp.float32), weights.astype(jnp.float32), precision=highest, preferred_element_type=jnp.float32)
    return mixed.reshape(field_in.shape)

def reference(right_side, start_field, coupling, mode_blocks):
    residual_zero = right_side - apply_operator(start_field, coupling, mode_blocks)
    krylov_basis = [residual_zero]
    for power_step in range(S):
        krylov_basis.append(apply_operator(krylov_basis[-1], coupling, mode_blocks))
    columns = krylov_basis[1:] + krylov_basis[:1]
    gram = jnp.block([[gram_block(left_col, right_col) for right_col in columns] for left_col in columns])
    factor = jnp.linalg.cholesky(gram)
    small_order = S * R
    coeffs = jax.scipy.linalg.solve_triangular(factor[:small_order, :small_order], factor[small_order:, :small_order].T, lower=True, trans=1)
    updated_field = start_field
    new_residual = residual_zero
    for power_step in range(S):
        block_weights = coeffs[power_step * R:(power_step + 1) * R]
        updated_field = updated_field + combine_blocks(krylov_basis[power_step], block_weights)
        new_residual = new_residual - combine_blocks(krylov_basis[power_step + 1], block_weights)
    return (updated_field, new_residual)
```

```python
import functools

import jax
import jax.numpy as jnp
from jax import lax
from jax.experimental import pallas as pl
from jax.experimental.pallas import tpu as pltpu
from jax.sharding import PartitionSpec as P

S = 4
MESH = pl.DeviceIdType.MESH
LANES = 128
KERNEL_VMEM = 24 * 2**20


def split(value):
    high = value.astype(jnp.bfloat16)
    low = (value - high.astype(jnp.float32)).astype(jnp.bfloat16)
    return high, low


def fold(product):
    half = product.shape[-1] // 2
    return product[..., :half] + product[..., half:]


def widen(piece, width):
    rows, cols = piece.shape
    if cols == width:
        return piece
    return jnp.concatenate([piece, jnp.zeros((rows, width - cols), piece.dtype)], axis=1)


def self_products(left, right):
    full = lax.dot_general(left, right, (((1,), (1,)), ((), ())), preferred_element_type=jnp.float32)
    return fold(full)


def unpack_gram(packed, r):
    def zeros(count):
        return jnp.zeros((r, count), jnp.float32)
    top, bottom = packed[:r], packed[r:]
    lines = [
        widen(top[:, :5 * r], LANES),
        widen(jnp.concatenate([zeros(r), bottom[:, :2 * r], zeros(r), bottom[:, 2 * r:3 * r]], axis=1), LANES),
        widen(jnp.concatenate([zeros(2 * r), top[:, 5 * r:8 * r]], axis=1), LANES),
        widen(bottom[:, 3 * r:8 * r], LANES),
        jnp.zeros((LANES - 4 * r, LANES), jnp.float32),
    ]
    upper = jnp.concatenate(lines, axis=0)
    row = lax.broadcasted_iota(jnp.int32, upper.shape, 0)
    col = lax.broadcasted_iota(jnp.int32, upper.shape, 1)
    last_row = jnp.logical_and(row >= 3 * r, row < 4 * r)
    last_col = jnp.logical_and(col >= 3 * r, col < 4 * r)
    direct = jnp.logical_or(last_row, jnp.logical_and(col >= row, jnp.logical_not(last_col)))
    return jnp.where(direct, upper, upper.T)


def basis_kernel(
    nx, ny, dims,
    rhs_hbm, start_hbm, coup_hbm, blocks_hbm,
    split_ref, gram_ref, start_ref,
    rhs_ref, coup_ref, blocks_ref, load_sem,
    field, rhs_rows, scale, lhs, weights, padded, kept, halo_x, halo_y,
    pair_buf, line_buf, cross_buf,
    halo_send, halo_recv, pair_sem, line_sem, cross_sem,
):
    gx, gy, rhs_count, modes, wide = dims
    rows = gy * rhs_count
    order = (S + 1) * rhs_count
    small = S * rhs_count
    ix, iy = lax.axis_index("ex"), lax.axis_index("ey")

    loads = [
        pltpu.make_async_copy(source, dest, load_sem.at[n])
        for n, (source, dest) in enumerate((
            (start_hbm, start_ref), (rhs_hbm, rhs_ref), (coup_hbm, coup_ref), (blocks_hbm, blocks_ref)))
    ]
    for load in loads:
        load.start()
    barrier = pltpu.get_barrier_semaphore()
    for d in range(1, nx):
        pl.semaphore_signal(barrier, inc=1, device_id={"ex": lax.rem(ix + d, nx)}, device_id_type=MESH)
    for d in range(1, ny):
        pl.semaphore_signal(barrier, inc=1, device_id={"ey": lax.rem(iy + d, ny)}, device_id_type=MESH)

    def unpack(source, write):
        def body(i, carry):
            for r in range(rhs_count):
                piece = source[i, :, r * modes:(r + 1) * modes]
                write(i, pl.ds(r, gy, stride=rhs_count), widen(piece, wide))
            return carry
        lax.fori_loop(0, gx, body, 0)

    def write_start(i, where, value):
        field[0, i, where, :] = value

    def write_rhs(i, where, value):
        rhs_rows[i, where, :] = value

    loads[0].wait()
    unpack(start_ref, write_start)

    def halo(t, way):
        source = field.at[t]
        if way == 0:
            part, target, dest = source.at[gx - 1], {"ex": lax.rem(ix + 1, nx)}, halo_x.at[t, 0]
        elif way == 1:
            part, target, dest = source.at[0], {"ex": lax.rem(ix + nx - 1, nx)}, halo_x.at[t, 1]
        elif way == 2:
            part, target, dest = source.at[:, rows - rhs_count:], {"ey": lax.rem(iy + 1, ny)}, halo_y.at[t, 0]
        else:
            part, target, dest = source.at[:, :rhs_count], {"ey": lax.rem(iy + ny - 1, ny)}, halo_y.at[t, 1]
        return pltpu.make_async_remote_copy(
            src_ref=part, dst_ref=dest, send_sem=halo_send.at[t, way], recv_sem=halo_recv.at[t, way],
            device_id=target, device_id_type=MESH,
        )

    sends = (ix < nx - 1, ix > 0, iy < ny - 1, iy > 0)
    receives = (ix > 0, ix < nx - 1, iy > 0, iy < ny - 1)
    odd = lax.rem(iy, 2) == 1
    starts = (
        (2, jnp.logical_and(sends[2], odd)), (3, sends[3]),
        (2, jnp.logical_and(sends[2], jnp.logical_not(odd))), (0, sends[0]), (1, sends[1]))

    def start_halos(t):
        for way, needed in starts:
            @pl.when(needed)
            def _():
                halo(t, way).start()

    pl.semaphore_wait(barrier, nx - 1 + ny - 1)
    start_halos(0)

    for load in loads[1:]:
        load.wait()
    unpack(rhs_ref, write_rhs)
    lhs[...] = jnp.zeros_like(lhs)
    padded[...] = jnp.zeros_like(padded)
    for first in (small - rhs_count, order + small - rhs_count):
        split_ref[first:first + rhs_count, :] = jnp.zeros((rhs_count, split_ref.shape[1]), jnp.bfloat16)
    for k in range(5):
        padded[:modes, :modes] = blocks_ref[k]
        high, low = split(padded[...])
        both = jnp.concatenate([high, low], axis=1)
        weights[2 * k * wide:(2 * k + 1) * wide, :] = both
        weights[(2 * k + 1) * wide:(2 * k + 2) * wide, :] = both

    def scale_body(i, carry):
        for k in range(5):
            for j in range(gy):
                scale[k, i, j * rhs_count:(j + 1) * rhs_count, :] = jnp.full(
                    (rhs_count, wide), coup_ref[k, i, j], jnp.float32)
        return carry
    lax.fori_loop(0, gx, scale_body, 0)

    def record(t, slot):
        for i in range(gx):
            for j in range(gy):
                e = i * gy + j
                high, low = split(field[t, i, j * rhs_count:(j + 1) * rhs_count, :])
                split_ref[slot * rhs_count:(slot + 1) * rhs_count, e * wide:(e + 1) * wide] = high
                split_ref[order + slot * rhs_count:order + (slot + 1) * rhs_count, e * wide:(e + 1) * wide] = low

    def put(k, i, lo_row, hi_row, value):
        high, low = split(value)
        lhs[i, lo_row:hi_row, 2 * k * wide:(2 * k + 1) * wide] = high
        lhs[i, lo_row:hi_row, (2 * k + 1) * wide:(2 * k + 2) * wide] = low

    def edge_dot(k, value):
        high, low = split(value)
        both = jnp.concatenate([high, low], axis=1)
        return fold(jnp.dot(both, weights[2 * k * wide:(2 * k + 2) * wide, :], preferred_element_type=jnp.float32))

    r = rhs_count
    for t in range(S + 1):
        if t > 0:
            start_halos(t)
        for i in range(gx):
            here = field[t, i]
            put(0, i, 0, rows, scale[0, i] * here)
            if i + 1 < gx:
                put(1, i + 1, 0, rows, scale[1, i + 1] * here)
            if i > 0:
                put(2, i - 1, 0, rows, scale[2, i - 1] * here)
            put(3, i, r, rows, scale[3, i, r:, :] * here[:rows - r])
            put(4, i, 0, rows - r, scale[4, i, :rows - r, :] * here[r:])
        product = fold(jnp.dot(
            lhs[...].reshape(gx * rows, 10 * wide), weights[...], preferred_element_type=jnp.float32
        )).reshape(gx, rows, wide)
        if t == 0:
            field[1] = rhs_rows[...] - product
        else:
            field[t + 1] = product
        if t > 0:
            record(t, (t - 2) % (S + 1))
        if t == S:
            early = self_products(split_ref[...], split_ref[...])
            early = early[:3 * r] + early[order:order + 3 * r]
            top = jnp.concatenate([early[:r], early[2 * r:, 2 * r:]], axis=1)
            bottom = jnp.concatenate([early[r:2 * r, r:3 * r], early[r:2 * r, 4 * r:]], axis=1)
            kept[:r, :] = widen(top, LANES)
            kept[r:, :] = widen(bottom, LANES)
        sign = -1.0 if t == 0 else 1.0

        for way in (0, 1):
            edge = 0 if way == 0 else gx - 1

            @pl.when(receives[way])
            def _():
                halo(t, way).wait_recv()
                add = edge_dot(1 + way, scale[1 + way, edge] * halo_x[t, way])
                field[t + 1, edge] = field[t + 1, edge] + sign * add
        for way in (2, 3):
            first = 0 if way == 2 else rows - r

            @pl.when(receives[way])
            def _():
                halo(t, way).wait_recv()
                value = scale[1 + way, :, first:first + r, :] * halo_y[t, way - 2]
                add = edge_dot(1 + way, value.reshape(gx * r, wide)).reshape(gx, r, wide)
                field[t + 1, :, first:first + r, :] = field[t + 1, :, first:first + r, :] + sign * add
    record(S + 1, S - 1)

    newest = jnp.concatenate([split_ref[small - r:small, :], split_ref[order + small - r:order + small, :]], axis=0)
    late = self_products(newest, split_ref[...])
    late = jnp.concatenate([kept[r:, :3 * r], late[:r] + late[r:]], axis=1)
    gram = jnp.concatenate([kept[:r, :], widen(late, LANES)], axis=0)

    unsent = []

    def reduce_over(count, mine, device, buf, sems, value):
        if count == 1:
            return value

        def copy(d, slot):
            return pltpu.make_async_remote_copy(
                src_ref=buf.at[mine], dst_ref=buf.at[slot], send_sem=sems.at[0, d - 1], recv_sem=sems.at[1, d - 1],
                device_id=device(lax.rem(mine + d, count)), device_id_type=MESH,
            )
        buf[mine] = value
        for d in range(1, count):
            copy(d, mine).start()
        for d in range(1, count):
            copy(d, lax.rem(mine + count - d, count)).wait_recv()
        total = buf[0]
        for s in range(1, count):
            total = total + buf[s]
        unsent.extend(copy(d, mine) for d in range(1, count))
        return total

    side = lax.rem(ix, 2)
    gram = reduce_over(2, side, lambda s: {"ex": ix - side + s}, pair_buf, pair_sem, gram)
    gram = reduce_over(nx // 2, ix // 2, lambda s: {"ex": 2 * s + side}, line_buf, line_sem, gram)
    gram = reduce_over(ny, iy, lambda s: {"ey": s}, cross_buf, cross_sem, gram)
    gram_ref[...] = gram
    for copy in unsent:
        copy.wait_send()

    for t in range(S + 1):
        for way in range(4):
            @pl.when(sends[way])
            def _():
                halo(t, way).wait_send()


PANEL = 4


def combine_kernel(
    dims, split_ref, gram_ref, start_ref, field_hbm, residual_hbm,
    field_out, residual_out, rows_ref, store_sem,
):
    gx, gy, rhs_count, modes, wide = dims
    order = (S + 1) * rhs_count
    small = S * rhs_count
    matrix = unpack_gram(gram_ref[...], rhs_count)
    tiles = [matrix[8 * b:8 * b + 8, :] for b in range(small // 8)]
    which = lax.broadcasted_iota(jnp.int32, (8, LANES), 0)
    for j in range(0, small, PANEL):
        b, s = divmod(j, 8)
        lines = [jnp.broadcast_to(tiles[b][s + q:s + q + 1, :], (8, LANES)) for q in range(PANEL)]
        pivots = [
            [jnp.broadcast_to(line[:, j + c:j + c + 1], (8, LANES)) for c in range(PANEL)] for line in lines]
        for q in range(PANEL):
            inverse = 1.0 / pivots[q][q]
            lines[q] = lines[q] * inverse
            for c in range(q + 1, PANEL):
                pivots[q][c] = pivots[q][c] * inverse
            for o in range(PANEL):
                if o != q:
                    factor = pivots[o][q]
                    lines[o] = lines[o] - factor * lines[q]
                    for c in range(q + 1, PANEL):
                        pivots[o][c] = pivots[o][c] - factor * pivots[q][c]
        updated = []
        for n, tile in enumerate(tiles):
            fresh = tile
            for q in range(PANEL):
                fresh = fresh - tile[:, j + q:j + q + 1] * lines[q]
            if n == b:
                for q in range(PANEL):
                    fresh = jnp.where(which == s + q, lines[q], fresh)
            updated.append(fresh)
        tiles = updated
    solved = jnp.concatenate(tiles, axis=0)
    turned = solved.T[small:order, :]
    zero = jnp.zeros((rhs_count, rhs_count), jnp.float32)
    forward = jnp.concatenate([turned[:, rhs_count:small], zero, turned[:, :rhs_count]], axis=1)
    backward = jnp.concatenate([-turned[:, :small], zero], axis=1)
    mixing = jnp.concatenate([forward, backward], axis=0)
    high, low = split(mixing)
    left = jnp.concatenate([
        jnp.concatenate([high, high], axis=1), jnp.concatenate([low, low], axis=1)], axis=0)
    stores = []
    for i in range(gx):
        lo, hi = i * gy * wide, (i + 1) * gy * wide
        mixed = jnp.dot(left, split_ref[:, lo:hi], preferred_element_type=jnp.float32)
        mixed = mixed[:2 * rhs_count] + mixed[2 * rhs_count:]
        zeroth = (split_ref[order - rhs_count:order, lo:hi].astype(jnp.float32)
                  + split_ref[2 * order - rhs_count:2 * order, lo:hi].astype(jnp.float32))
        first = mixed[:rhs_count]
        second = mixed[rhs_count:] + zeroth
        for j in range(gy):
            rows_ref[0, i, j * rhs_count:(j + 1) * rhs_count, :] = first[:, j * wide:(j + 1) * wide]
            rows_ref[1, i, j * rhs_count:(j + 1) * rhs_count, :] = second[:, j * wide:(j + 1) * wide]
        for r in range(rhs_count):
            at = slice(r * modes, (r + 1) * modes)
            where = pl.ds(r, gy, stride=rhs_count)
            field_out[i, :, at] = start_ref[i, :, at] + rows_ref[0, i, where, :][:, :modes]
            residual_out[i, :, at] = rows_ref[1, i, where, :][:, :modes]
        for n, (source, dest) in enumerate(((field_out, field_hbm), (residual_out, residual_hbm))):
            stores.append(pltpu.make_async_copy(source.at[i], dest.at[i], store_sem.at[n, i]))
            stores[-1].start()
    for store in stores:
        store.wait()


def per_device(nx, ny, right_side, start_field, coupling, mode_blocks):
    gx, gy, row_width = right_side.shape
    modes = mode_blocks.shape[1]
    rhs_count = row_width // modes
    wide = -(-modes // LANES) * LANES
    dims = (gx, gy, rhs_count, modes, wide)
    rows = gy * rhs_count
    order, small = (S + 1) * rhs_count, S * rhs_count
    vmem = pl.BlockSpec(memory_space=pltpu.VMEM)
    anywhere = pl.BlockSpec(memory_space=pl.ANY)
    dma = pltpu.SemaphoreType.DMA
    f32, bf16 = jnp.float32, jnp.bfloat16
    slab = (gx, gy, row_width)
    split_shape = (2 * order, gx * gy * wide)
    packed = (2 * rhs_count, LANES)
    hbm_args = [
        pltpu.with_memory_space_constraint(x, pltpu.HBM)
        for x in (right_side, start_field, coupling, mode_blocks)]
    pieces, gram, start_held = pl.pallas_call(
        functools.partial(basis_kernel, nx, ny, dims),
        out_shape=(jax.ShapeDtypeStruct(split_shape, bf16), jax.ShapeDtypeStruct(packed, f32),
                   jax.ShapeDtypeStruct(slab, f32)),
        in_specs=[anywhere] * 4,
        out_specs=(vmem, vmem, vmem),
        scratch_shapes=[
            pltpu.VMEM(slab, f32),
            pltpu.SMEM((5, gx, gy), f32),
            pltpu.VMEM(mode_blocks.shape, f32),
            dma((4,)),
            pltpu.VMEM((S + 2, gx, rows, wide), f32),
            pltpu.VMEM((gx, rows, wide), f32),
            pltpu.VMEM((5, gx, rows, wide), f32),
            pltpu.VMEM((gx, rows, 10 * wide), bf16),
            pltpu.VMEM((10 * wide, 2 * wide), bf16),
            pltpu.VMEM((wide, wide), f32),
            pltpu.VMEM(packed, f32),
            pltpu.VMEM((S + 1, 2, rows, wide), f32),
            pltpu.VMEM((S + 1, 2, gx, rhs_count, wide), f32),
            pltpu.VMEM((2,) + packed, f32),
            pltpu.VMEM((nx // 2,) + packed, f32),
            pltpu.VMEM((ny,) + packed, f32),
            dma((S + 1, 4)),
            dma((S + 1, 4)),
            dma((2, 1)),
            dma((2, max(nx // 2 - 1, 1))),
            dma((2, max(ny - 1, 1))),
        ],
        compiler_params=pltpu.CompilerParams(collective_id=0, has_side_effects=True, vmem_limit_bytes=KERNEL_VMEM),
    )(*hbm_args)
    out = jax.ShapeDtypeStruct(slab, f32)
    return pl.pallas_call(
        functools.partial(combine_kernel, dims),
        out_shape=(out, out),
        in_specs=[vmem, vmem, vmem],
        out_specs=(anywhere, anywhere),
        scratch_shapes=[
            pltpu.VMEM(slab, f32),
            pltpu.VMEM(slab, f32),
            pltpu.VMEM((2, gx, rows, wide), f32),
            dma((2, gx)),
        ],
        compiler_params=pltpu.CompilerParams(vmem_limit_bytes=KERNEL_VMEM),
    )(pieces, gram, start_held)


def solution(mesh):
    return jax.shard_map(
        functools.partial(per_device, mesh.shape["ex"], mesh.shape["ey"]),
        mesh=mesh,
        in_specs=(P("ex", "ey", None), P("ex", "ey", None), P(None, "ex", "ey"), P()),
        out_specs=(P("ex", "ey", None), P("ex", "ey", None)),
        check_vma=False,
    )
```

```python
import functools

import jax
import jax.numpy as jnp
from jax import lax
from jax.experimental import pallas as pl
from jax.experimental.pallas import tpu as pltpu
from jax.sharding import PartitionSpec as P

S = 4
MESH = pl.DeviceIdType.MESH
LANES = 128
KERNEL_VMEM = 24 * 2**20
PANEL = 8


def split(value):
    high = value.astype(jnp.bfloat16)
    low = (value - high.astype(jnp.float32)).astype(jnp.bfloat16)
    return high, low


def fold(product):
    half = product.shape[-1] // 2
    return product[..., :half] + product[..., half:]


def widen(piece, width):
    rows, cols = piece.shape
    if cols == width:
        return piece
    return jnp.concatenate([piece, jnp.zeros((rows, width - cols), piece.dtype)], axis=1)


def self_products(left, right):
    full = lax.dot_general(left, right, (((1,), (1,)), ((), ())), preferred_element_type=jnp.float32)
    return fold(full)


def thirds(value):
    high = value.astype(jnp.bfloat16)
    rest = value - high.astype(jnp.float32)
    middle = rest.astype(jnp.bfloat16)
    return high, middle, (rest - middle.astype(jnp.float32)).astype(jnp.bfloat16)


def left_form(value):
    high, middle, low = thirds(value)
    return jnp.concatenate([high, high, middle, high, middle, low], axis=1)


def right_form(value):
    high, middle, low = thirds(value)
    return jnp.concatenate([high, middle, high, low, middle, high], axis=0)


def dot_forms(left, right):
    return jnp.dot(left, right, preferred_element_type=jnp.float32)


def at_rows(piece, first, height):
    parts = [piece, jnp.zeros((height - first - piece.shape[0], piece.shape[1]), piece.dtype)]
    if first:
        parts.insert(0, jnp.zeros((first, piece.shape[1]), piece.dtype))
    return jnp.concatenate(parts, axis=0)


def panel_lines(tile, s, first):
    lines = [jnp.broadcast_to(tile[s + q:s + q + 1, :], (8, LANES)) for q in range(PANEL)]
    pivots = [
        [jnp.broadcast_to(line[:, first + c:first + c + 1], (8, LANES)) for c in range(PANEL)] for line in lines]
    for q in range(PANEL):
        inverse = 1.0 / pivots[q][q]
        lines[q] = lines[q] * inverse
        for c in range(q + 1, PANEL):
            pivots[q][c] = pivots[q][c] * inverse
        for o in range(PANEL):
            if o != q:
                factor = pivots[o][q]
                lines[o] = lines[o] - factor * lines[q]
                for c in range(q + 1, PANEL):
                    pivots[o][c] = pivots[o][c] - factor * pivots[q][c]
    return lines


def eliminate(tile, lines, first):
    fresh = tile
    for q in range(PANEL):
        fresh = fresh - tile[:, first + q:first + q + 1] * lines[q]
    return fresh


def factor_early(early, r):
    row = lax.broadcasted_iota(jnp.int32, early.shape, 0)
    col = lax.broadcasted_iota(jnp.int32, early.shape, 1)
    matrix = jnp.where(col < 3 * r, early, (col == row + 4 * r).astype(jnp.float32))
    tiles = [matrix[8 * b:8 * b + 8, :] for b in range(3 * r // 8)]
    scaled = list(tiles)
    which = lax.broadcasted_iota(jnp.int32, (8, LANES), 0)
    for j in range(0, 3 * r, PANEL):
        b, s = divmod(j, 8)
        lines = panel_lines(tiles[b], s, j)
        for q in range(PANEL):
            scaled[b] = jnp.where(which == s + q, lines[q], scaled[b])
        if s + PANEL < 8:
            tiles[b] = jnp.where(which >= s + PANEL, eliminate(tiles[b], lines, j), tiles[b])
        for n in range(b + 1, len(tiles)):
            tiles[n] = eliminate(tiles[n], lines, j)
    lower = jnp.concatenate(tiles, axis=0)
    both = left_form(jnp.concatenate([lower, jnp.concatenate(scaled, axis=0)], axis=0))
    zeroth = dot_forms(both[3 * r:], right_form(at_rows(early[:, 4 * r:5 * r], 4 * r, LANES)))
    upper = at_rows(lower, 0, LANES).T[4 * r:7 * r]
    return both, left_form(upper), zeroth


def finish_solve(both, upper, zeroth, late, r):
    blocks = [late[:, k * r:(k + 1) * r] for k in range(5)]
    turned = dot_forms(both, right_form(at_rows(jnp.concatenate(blocks[:3], axis=0), 4 * r, LANES)))
    first = widen(at_rows(turned[:3 * r], 0, LANES), LANES).T[:r]
    right = at_rows(jnp.concatenate([turned[3 * r:], zeroth], axis=1), 0, LANES)
    rest = dot_forms(jnp.concatenate([upper, left_form(first)], axis=0), right_form(right))
    last = jnp.concatenate([blocks[3], widen(at_rows(blocks[4], 0, LANES), LANES).T[:r, :r]], axis=1)
    rest = jnp.concatenate([rest[:3 * r], last - rest[3 * r:]], axis=0)
    rest = widen(rest, LANES)
    tiles = [rest[8 * b:8 * b + 8, :] for b in range(4 * r // 8)]
    which = lax.broadcasted_iota(jnp.int32, (8, LANES), 0)
    for j in range(0, r, PANEL):
        b, s = divmod(3 * r + j, 8)
        lines = panel_lines(tiles[b], s, j)
        tiles = [eliminate(tile, lines, j) for tile in tiles]
        for q in range(PANEL):
            tiles[b] = jnp.where(which == s + q, lines[q], tiles[b])
    return jnp.concatenate(tiles, axis=0).T[r:2 * r, :]


def basis_kernel(
    nx, ny, dims,
    rhs_hbm, start_hbm, coup_hbm, blocks_hbm,
    split_ref, mixing_ref, start_ref,
    rhs_ref, coup_ref, blocks_ref, load_sem,
    field, rhs_rows, scale, lhs, weights, padded, halo_x, halo_y, raw_x, raw_y,
    early_pair, early_line, early_cross, late_pair, late_line, late_cross,
    both_ref, upper_ref, zeroth_ref, halo_send, halo_recv,
    early_pair_sem, early_line_sem, early_cross_sem, late_pair_sem, late_line_sem, late_cross_sem,
):
    gx, gy, rhs_count, modes, wide = dims
    rows = gy * rhs_count
    order = (S + 1) * rhs_count
    small = S * rhs_count
    ix, iy = lax.axis_index("ex"), lax.axis_index("ey")

    barrier = pltpu.get_barrier_semaphore()
    for d in range(1, nx):
        pl.semaphore_signal(barrier, inc=1, device_id={"ex": lax.rem(ix + d, nx)}, device_id_type=MESH)
    for d in range(1, ny):
        pl.semaphore_signal(barrier, inc=1, device_id={"ey": lax.rem(iy + d, ny)}, device_id_type=MESH)
    loads = [
        pltpu.make_async_copy(source, dest, load_sem.at[n])
        for n, (source, dest) in enumerate((
            (start_hbm, start_ref), (rhs_hbm, rhs_ref), (coup_hbm, coup_ref), (blocks_hbm, blocks_ref)))
    ]
    for load in loads:
        load.start()

    def unpack(source, write):
        def body(i, carry):
            for r in range(rhs_count):
                piece = source[i, :, r * modes:(r + 1) * modes]
                write(i, pl.ds(r, gy, stride=rhs_count), widen(piece, wide))
            return carry
        lax.fori_loop(0, gx, body, 0)

    def write_start(i, where, value):
        field[0, i, where, :] = value

    def write_rhs(i, where, value):
        rhs_rows[i, where, :] = value

    def halo(t, way):
        target = ({"ex": lax.rem(ix + 1, nx)}, {"ex": lax.rem(ix + nx - 1, nx)},
                  {"ey": lax.rem(iy + 1, ny)}, {"ey": lax.rem(iy + ny - 1, ny)})[way]
        if t == 0:
            part = (start_hbm.at[gx - 1], start_hbm.at[0], start_hbm.at[:, gy - 1], start_hbm.at[:, 0])[way]
            dest = raw_x.at[way] if way < 2 else raw_y.at[way - 2]
        else:
            source = field.at[t]
            part = (source.at[gx - 1], source.at[0], source.at[:, rows - rhs_count:], source.at[:, :rhs_count])[way]
            dest = halo_x.at[t, way] if way < 2 else halo_y.at[t, way - 2]
        return pltpu.make_async_remote_copy(
            src_ref=part, dst_ref=dest, send_sem=halo_send.at[t, way], recv_sem=halo_recv.at[t, way],
            device_id=target, device_id_type=MESH,
        )

    sends = (ix < nx - 1, ix > 0, iy < ny - 1, iy > 0)
    receives = (ix > 0, ix < nx - 1, iy > 0, iy < ny - 1)
    odd = lax.rem(iy, 2) == 1
    starts = (
        (2, jnp.logical_and(sends[2], odd)), (3, sends[3]),
        (2, jnp.logical_and(sends[2], jnp.logical_not(odd))), (0, sends[0]), (1, sends[1]))

    def start_halos(t):
        for way, needed in starts:
            @pl.when(needed)
            def _():
                halo(t, way).start()

    pl.semaphore_wait(barrier, nx - 1 + ny - 1)
    start_halos(0)

    loads[0].wait()
    unpack(start_ref, write_start)
    for load in loads[1:]:
        load.wait()
    unpack(rhs_ref, write_rhs)
    for i, k in ((0, 1), (gx - 1, 2)):
        lhs[i, :, 2 * k * wide:(2 * k + 2) * wide] = jnp.zeros((rows, 2 * wide), jnp.bfloat16)
    for k, first in ((3, 0), (4, rows - rhs_count)):
        for i in range(gx):
            lhs[i, first:first + rhs_count, 2 * k * wide:(2 * k + 2) * wide] = jnp.zeros(
                (rhs_count, 2 * wide), jnp.bfloat16)
    padded[...] = jnp.zeros_like(padded)
    for first in (small - rhs_count, order + small - rhs_count):
        split_ref[first:first + rhs_count, :] = jnp.zeros((rhs_count, split_ref.shape[1]), jnp.bfloat16)
    for k in range(5):
        padded[:modes, :modes] = blocks_ref[k]
        high, low = split(padded[...])
        both = jnp.concatenate([high, low], axis=1)
        weights[2 * k * wide:(2 * k + 1) * wide, :] = both
        weights[(2 * k + 1) * wide:(2 * k + 2) * wide, :] = both

    def scale_body(i, carry):
        for k in range(5):
            for j in range(gy):
                scale[k, i, j * rhs_count:(j + 1) * rhs_count, :] = jnp.full(
                    (rhs_count, wide), coup_ref[k, i, j], jnp.float32)
        return carry
    lax.fori_loop(0, gx, scale_body, 0)

    def record(t, slot):
        for i in range(gx):
            for j in range(gy):
                e = i * gy + j
                high, low = split(field[t, i, j * rhs_count:(j + 1) * rhs_count, :])
                split_ref[slot * rhs_count:(slot + 1) * rhs_count, e * wide:(e + 1) * wide] = high
                split_ref[order + slot * rhs_count:order + (slot + 1) * rhs_count, e * wide:(e + 1) * wide] = low

    def put(k, i, lo_row, hi_row, value):
        high, low = split(value)
        lhs[i, lo_row:hi_row, 2 * k * wide:(2 * k + 1) * wide] = high
        lhs[i, lo_row:hi_row, (2 * k + 1) * wide:(2 * k + 2) * wide] = low

    def edge_dot(k, value):
        high, low = split(value)
        both = jnp.concatenate([high, low], axis=1)
        return fold(jnp.dot(both, weights[2 * k * wide:(2 * k + 2) * wide, :], preferred_element_type=jnp.float32))

    unsent = []

    def exchange(count, mine, device, buf, sems):
        def copy(d, slot):
            return pltpu.make_async_remote_copy(
                src_ref=buf.at[mine], dst_ref=buf.at[slot], send_sem=sems.at[0, d - 1], recv_sem=sems.at[1, d - 1],
                device_id=device(lax.rem(mine + d, count)), device_id_type=MESH,
            )

        def begin(value):
            buf[mine] = value
            for d in range(1, count):
                copy(d, mine).start()
            unsent.extend(copy(d, mine) for d in range(1, count))

        def end():
            for d in range(1, count):
                copy(d, lax.rem(mine + count - d, count)).wait_recv()
            total = buf[0]
            for s in range(1, count):
                total = total + buf[s]
            return total
        return begin, end

    side = lax.rem(ix, 2)

    def stages(pair, line, cross, pair_sem, line_sem, cross_sem):
        return (
            exchange(2, side, lambda s: {"ex": ix - side + s}, pair, pair_sem),
            exchange(nx // 2, ix // 2, lambda s: {"ex": 2 * s + side}, line, line_sem),
            exchange(ny, iy, lambda s: {"ey": s}, cross, cross_sem),
        )
    early_stages = stages(early_pair, early_line, early_cross, early_pair_sem, early_line_sem, early_cross_sem)
    late_stages = stages(late_pair, late_line, late_cross, late_pair_sem, late_line_sem, late_cross_sem)

    r = rhs_count
    for t in range(S + 1):
        if t > 0:
            start_halos(t)
        for i in range(gx):
            here = field[t, i]
            put(0, i, 0, rows, scale[0, i] * here)
            if i + 1 < gx:
                put(1, i + 1, 0, rows, scale[1, i + 1] * here)
            if i > 0:
                put(2, i - 1, 0, rows, scale[2, i - 1] * here)
            put(3, i, r, rows, scale[3, i, r:, :] * here[:rows - r])
            put(4, i, 0, rows - r, scale[4, i, :rows - r, :] * here[r:])
        product = fold(jnp.dot(
            lhs[...].reshape(gx * rows, 10 * wide), weights[...], preferred_element_type=jnp.float32
        )).reshape(gx, rows, wide)
        if t == 0:
            field[1] = rhs_rows[...] - product
        else:
            field[t + 1] = product
        if t > 0:
            record(t, (t - 2) % (S + 1))
        if t == S:
            early = self_products(split_ref[...], split_ref[...])
            early_stages[0][0](widen(early[:3 * r] + early[order:order + 3 * r], LANES))
            early_stages[1][0](early_stages[0][1]())
        sign = -1.0 if t == 0 else 1.0

        for way in (0, 1):
            edge = 0 if way == 0 else gx - 1

            @pl.when(receives[way])
            def _():
                halo(t, way).wait_recv()
                if t == 0:
                    for s in range(rhs_count):
                        halo_x[0, way, pl.ds(s, gy, stride=rhs_count), :] = widen(
                            raw_x[way, :, s * modes:(s + 1) * modes], wide)
                add = edge_dot(1 + way, scale[1 + way, edge] * halo_x[t, way])
                field[t + 1, edge] = field[t + 1, edge] + sign * add
        for way in (2, 3):
            first = 0 if way == 2 else rows - r

            @pl.when(receives[way])
            def _():
                halo(t, way).wait_recv()
                if t == 0:
                    for s in range(rhs_count):
                        halo_y[0, way - 2, :, s, :] = widen(raw_y[way - 2, :, s * modes:(s + 1) * modes], wide)
                value = scale[1 + way, :, first:first + r, :] * halo_y[t, way - 2]
                add = edge_dot(1 + way, value.reshape(gx * r, wide)).reshape(gx, r, wide)
                field[t + 1, :, first:first + r, :] = field[t + 1, :, first:first + r, :] + sign * add
    record(S + 1, S - 1)

    newest = jnp.concatenate([split_ref[small - r:small, :], split_ref[order + small - r:order + small, :]], axis=0)
    late = self_products(split_ref[...], newest)
    late = late[:order] + late[order:]
    late = jnp.concatenate([late[k * r:(k + 1) * r] for k in range(S + 1)], axis=1)
    late_stages[0][0](widen(late, LANES))
    late_stages[1][0](late_stages[0][1]())
    early_stages[2][0](early_stages[1][1]())
    late_stages[2][0](late_stages[1][1]())
    both, upper, zeroth = factor_early(early_stages[2][1](), r)
    both_ref[...] = both
    upper_ref[...] = upper
    zeroth_ref[...] = widen(zeroth, LANES)

    @pl.when(ix >= 0)
    def _():
        late = late_stages[2][1]()
        mixing_ref[...] = widen(
            finish_solve(both_ref[...], upper_ref[...], zeroth_ref[:, :r], late, r), LANES)
    for copy in unsent:
        copy.wait_send()

    for t in range(S + 1):
        for way in range(4):
            @pl.when(sends[way])
            def _():
                halo(t, way).wait_send()


def combine_kernel(
    dims, split_ref, mixing_ref, start_ref, field_hbm, residual_hbm,
    field_out, residual_out, rows_ref, store_sem,
):
    gx, gy, rhs_count, modes, wide = dims
    order = (S + 1) * rhs_count
    small = S * rhs_count
    turned = mixing_ref[:, :small]
    zero = jnp.zeros((rhs_count, rhs_count), jnp.float32)
    forward = jnp.concatenate([turned[:, rhs_count:small], zero, turned[:, :rhs_count]], axis=1)
    backward = jnp.concatenate([-turned[:, :small], zero], axis=1)
    mixing = jnp.concatenate([forward, backward], axis=0)
    high, low = split(mixing)
    left = jnp.concatenate([
        jnp.concatenate([high, high], axis=1), jnp.concatenate([low, low], axis=1)], axis=0)
    stores = []
    for i in range(gx):
        lo, hi = i * gy * wide, (i + 1) * gy * wide
        mixed = jnp.dot(left, split_ref[:, lo:hi], preferred_element_type=jnp.float32)
        mixed = mixed[:2 * rhs_count] + mixed[2 * rhs_count:]
        zeroth = (split_ref[order - rhs_count:order, lo:hi].astype(jnp.float32)
                  + split_ref[2 * order - rhs_count:2 * order, lo:hi].astype(jnp.float32))
        first = mixed[:rhs_count]
        second = mixed[rhs_count:] + zeroth
        for j in range(gy):
            rows_ref[0, i, j * rhs_count:(j + 1) * rhs_count, :] = first[:, j * wide:(j + 1) * wide]
            rows_ref[1, i, j * rhs_count:(j + 1) * rhs_count, :] = second[:, j * wide:(j + 1) * wide]
        for r in range(rhs_count):
            at = slice(r * modes, (r + 1) * modes)
            where = pl.ds(r, gy, stride=rhs_count)
            field_out[i, :, at] = start_ref[i, :, at] + rows_ref[0, i, where, :][:, :modes]
            residual_out[i, :, at] = rows_ref[1, i, where, :][:, :modes]
        for n, (source, dest) in enumerate(((field_out, field_hbm), (residual_out, residual_hbm))):
            stores.append(pltpu.make_async_copy(source.at[i], dest.at[i], store_sem.at[n, i]))
            stores[-1].start()
    for store in stores:
        store.wait()


def per_device(nx, ny, right_side, start_field, coupling, mode_blocks):
    gx, gy, row_width = right_side.shape
    modes = mode_blocks.shape[1]
    rhs_count = row_width // modes
    wide = -(-modes // LANES) * LANES
    dims = (gx, gy, rhs_count, modes, wide)
    rows = gy * rhs_count
    order, small = (S + 1) * rhs_count, S * rhs_count
    vmem = pl.BlockSpec(memory_space=pltpu.VMEM)
    anywhere = pl.BlockSpec(memory_space=pl.ANY)
    dma = pltpu.SemaphoreType.DMA
    f32, bf16 = jnp.float32, jnp.bfloat16
    slab = (gx, gy, row_width)
    split_shape = (2 * order, gx * gy * wide)
    early, late = ((S - 1) * rhs_count, LANES), (rhs_count, LANES)
    hbm_args = [
        pltpu.with_memory_space_constraint(x, pltpu.HBM)
        for x in (right_side, start_field, coupling, mode_blocks)]
    pieces, mixing, start_held = pl.pallas_call(
        functools.partial(basis_kernel, nx, ny, dims),
        out_shape=(jax.ShapeDtypeStruct(split_shape, bf16), jax.ShapeDtypeStruct(late, f32),
                   jax.ShapeDtypeStruct(slab, f32)),
        in_specs=[anywhere] * 4,
        out_specs=(vmem, vmem, vmem),
        scratch_shapes=[
            pltpu.VMEM(slab, f32),
            pltpu.SMEM((5, gx, gy), f32),
            pltpu.VMEM(mode_blocks.shape, f32),
            dma((4,)),
            pltpu.VMEM((S + 2, gx, rows, wide), f32),
            pltpu.VMEM((gx, rows, wide), f32),
            pltpu.VMEM((5, gx, rows, wide), f32),
            pltpu.VMEM((gx, rows, 10 * wide), bf16),
            pltpu.VMEM((10 * wide, 2 * wide), bf16),
            pltpu.VMEM((wide, wide), f32),
            pltpu.VMEM((S + 1, 2, rows, wide), f32),
            pltpu.VMEM((S + 1, 2, gx, rhs_count, wide), f32),
            pltpu.VMEM((2, gy, row_width), f32),
            pltpu.VMEM((2, gx, row_width), f32),
            *[pltpu.VMEM((count,) + shape, f32) for shape in (early, late) for count in (2, nx // 2, ny)],
            pltpu.VMEM((2 * early[0], 6 * LANES), bf16),
            pltpu.VMEM((early[0], 6 * LANES), bf16),
            pltpu.VMEM(early, f32),
            dma((S + 1, 4)),
            dma((S + 1, 4)),
            *[dma((2, max(count - 1, 1))) for _ in range(2) for count in (2, nx // 2, ny)],
        ],
        compiler_params=pltpu.CompilerParams(collective_id=0, has_side_effects=True, vmem_limit_bytes=KERNEL_VMEM),
    )(*hbm_args)
    out = jax.ShapeDtypeStruct(slab, f32)
    return pl.pallas_call(
        functools.partial(combine_kernel, dims),
        out_shape=(out, out),
        in_specs=[vmem, vmem, vmem],
        out_specs=(anywhere, anywhere),
        scratch_shapes=[
            pltpu.VMEM(slab, f32),
            pltpu.VMEM(slab, f32),
            pltpu.VMEM((2, gx, rows, wide), f32),
            dma((2, gx)),
        ],
        compiler_params=pltpu.CompilerParams(vmem_limit_bytes=KERNEL_VMEM),
    )(pieces, mixing, start_held)


def solution(mesh):
    return jax.shard_map(
        functools.partial(per_device, mesh.shape["ex"], mesh.shape["ey"]),
        mesh=mesh,
        in_specs=(P("ex", "ey", None), P("ex", "ey", None), P(None, "ex", "ey"), P()),
        out_specs=(P("ex", "ey", None), P("ex", "ey", None)),
        check_vma=False,
    )
```

```python
import functools

import jax
import jax.numpy as jnp
from jax import lax
from jax.experimental import pallas as pl
from jax.experimental.pallas import tpu as pltpu
from jax.sharding import PartitionSpec as P

S = 4
MESH = pl.DeviceIdType.MESH
LANES = 128
KERNEL_VMEM = 24 * 2**20
PANEL = 8


def split(value):
    high = value.astype(jnp.bfloat16)
    low = (value - high.astype(jnp.float32)).astype(jnp.bfloat16)
    return high, low


def fold(product):
    half = product.shape[-1] // 2
    return product[..., :half] + product[..., half:]


def widen(piece, width):
    rows, cols = piece.shape
    if cols == width:
        return piece
    return jnp.concatenate([piece, jnp.zeros((rows, width - cols), piece.dtype)], axis=1)


def self_products(left, right):
    full = lax.dot_general(left, right, (((1,), (1,)), ((), ())), preferred_element_type=jnp.float32)
    return fold(full)


def thirds(value):
    high = value.astype(jnp.bfloat16)
    rest = value - high.astype(jnp.float32)
    middle = rest.astype(jnp.bfloat16)
    return high, middle, (rest - middle.astype(jnp.float32)).astype(jnp.bfloat16)


def left_form(value):
    high, middle, low = thirds(value)
    return jnp.concatenate([high, high, middle, high, middle, low], axis=1)


def right_form(value):
    high, middle, low = thirds(value)
    return jnp.concatenate([high, middle, high, low, middle, high], axis=0)


def dot_forms(left, right):
    return jnp.dot(left, right, preferred_element_type=jnp.float32)


def at_rows(piece, first, height):
    parts = [piece, jnp.zeros((height - first - piece.shape[0], piece.shape[1]), piece.dtype)]
    if first:
        parts.insert(0, jnp.zeros((first, piece.shape[1]), piece.dtype))
    return jnp.concatenate(parts, axis=0)


def panel_lines(tile, s, first):
    lines = [jnp.broadcast_to(tile[s + q:s + q + 1, :], (8, LANES)) for q in range(PANEL)]
    pivots = [
        [jnp.broadcast_to(line[:, first + c:first + c + 1], (8, LANES)) for c in range(PANEL)] for line in lines]
    for q in range(PANEL):
        inverse = 1.0 / pivots[q][q]
        lines[q] = lines[q] * inverse
        for c in range(q + 1, PANEL):
            pivots[q][c] = pivots[q][c] * inverse
        for o in range(PANEL):
            if o != q:
                factor = pivots[o][q]
                lines[o] = lines[o] - factor * lines[q]
                for c in range(q + 1, PANEL):
                    pivots[o][c] = pivots[o][c] - factor * pivots[q][c]
    return lines


def eliminate(tile, lines, first):
    fresh = tile
    for q in range(PANEL):
        fresh = fresh - tile[:, first + q:first + q + 1] * lines[q]
    return fresh


def factor_early(early, r):
    row = lax.broadcasted_iota(jnp.int32, early.shape, 0)
    col = lax.broadcasted_iota(jnp.int32, early.shape, 1)
    matrix = jnp.where(col < 3 * r, early, (col == row + 4 * r).astype(jnp.float32))
    tiles = [matrix[8 * b:8 * b + 8, :] for b in range(3 * r // 8)]
    scaled = list(tiles)
    which = lax.broadcasted_iota(jnp.int32, (8, LANES), 0)
    for j in range(0, 3 * r, PANEL):
        b, s = divmod(j, 8)
        lines = panel_lines(tiles[b], s, j)
        for q in range(PANEL):
            scaled[b] = jnp.where(which == s + q, lines[q], scaled[b])
        if s + PANEL < 8:
            tiles[b] = jnp.where(which >= s + PANEL, eliminate(tiles[b], lines, j), tiles[b])
        for n in range(b + 1, len(tiles)):
            tiles[n] = eliminate(tiles[n], lines, j)
    lower = jnp.concatenate(tiles, axis=0)
    both = left_form(jnp.concatenate([lower, jnp.concatenate(scaled, axis=0)], axis=0))
    zeroth = dot_forms(both[3 * r:], right_form(at_rows(early[:, 4 * r:5 * r], 4 * r, LANES)))
    upper = at_rows(lower, 0, LANES).T[4 * r:7 * r]
    return both, left_form(upper), zeroth


def finish_solve(both, upper, zeroth, late, r):
    blocks = [late[:, k * r:(k + 1) * r] for k in range(5)]
    turned = dot_forms(both, right_form(at_rows(jnp.concatenate(blocks[:3], axis=0), 4 * r, LANES)))
    first = widen(at_rows(turned[:3 * r], 0, LANES), LANES).T[:r]
    right = at_rows(jnp.concatenate([turned[3 * r:], zeroth], axis=1), 0, LANES)
    rest = dot_forms(jnp.concatenate([upper, left_form(first)], axis=0), right_form(right))
    last = jnp.concatenate([blocks[3], widen(at_rows(blocks[4], 0, LANES), LANES).T[:r, :r]], axis=1)
    rest = jnp.concatenate([rest[:3 * r], last - rest[3 * r:]], axis=0)
    rest = widen(rest, LANES)
    tiles = [rest[8 * b:8 * b + 8, :] for b in range(4 * r // 8)]
    which = lax.broadcasted_iota(jnp.int32, (8, LANES), 0)
    for j in range(0, r, PANEL):
        b, s = divmod(3 * r + j, 8)
        lines = panel_lines(tiles[b], s, j)
        tiles = [eliminate(tile, lines, j) for tile in tiles]
        for q in range(PANEL):
            tiles[b] = jnp.where(which == s + q, lines[q], tiles[b])
    return jnp.concatenate(tiles, axis=0).T[r:2 * r, :]


def basis_kernel(
    nx, ny, dims,
    rhs_hbm, start_hbm, coup_hbm, blocks_hbm,
    split_ref, mixing_ref, start_ref,
    rhs_ref, coup_ref, blocks_ref, load_sem,
    field, rhs_rows, scale, lhs, weights, padded, halo_x, halo_y, raw_x, raw_y,
    early_pair, early_line, early_cross, late_pair, late_line, late_cross,
    both_ref, upper_ref, zeroth_ref, halo_send, halo_recv,
    early_pair_sem, early_line_sem, early_cross_sem, late_pair_sem, late_line_sem, late_cross_sem,
):
    gx, gy, rhs_count, modes, wide = dims
    rows = gy * rhs_count
    order = (S + 1) * rhs_count
    small = S * rhs_count
    ix, iy = lax.axis_index("ex"), lax.axis_index("ey")

    barrier = pltpu.get_barrier_semaphore()
    greeted = [d for d in range(1, nx) if d in (1, nx - 1) or d % 2 == 0]
    for d in greeted:
        pl.semaphore_signal(barrier, inc=1, device_id={"ex": lax.rem(ix + d, nx)}, device_id_type=MESH)
    for d in range(1, ny):
        pl.semaphore_signal(barrier, inc=1, device_id={"ey": lax.rem(iy + d, ny)}, device_id_type=MESH)
    loads = [
        pltpu.make_async_copy(source, dest, load_sem.at[n])
        for n, (source, dest) in enumerate((
            (start_hbm, start_ref), (rhs_hbm, rhs_ref), (coup_hbm, coup_ref), (blocks_hbm, blocks_ref)))
    ]
    for load in loads:
        load.start()

    def unpack(source, write):
        def body(i, carry):
            for r in range(rhs_count):
                piece = source[i, :, r * modes:(r + 1) * modes]
                write(i, pl.ds(r, gy, stride=rhs_count), widen(piece, wide))
            return carry
        lax.fori_loop(0, gx, body, 0)

    def write_start(i, where, value):
        field[0, i, where, :] = value

    def write_rhs(i, where, value):
        rhs_rows[i, where, :] = value

    def halo(t, way):
        target = ({"ex": lax.rem(ix + 1, nx)}, {"ex": lax.rem(ix + nx - 1, nx)},
                  {"ey": lax.rem(iy + 1, ny)}, {"ey": lax.rem(iy + ny - 1, ny)})[way]
        if t == 0:
            part = (start_hbm.at[gx - 1], start_hbm.at[0], start_hbm.at[:, gy - 1], start_hbm.at[:, 0])[way]
            dest = raw_x.at[way] if way < 2 else raw_y.at[way - 2]
        else:
            source = field.at[t]
            part = (source.at[gx - 1], source.at[0], source.at[:, rows - rhs_count:], source.at[:, :rhs_count])[way]
            dest = halo_x.at[t, way] if way < 2 else halo_y.at[t, way - 2]
        return pltpu.make_async_remote_copy(
            src_ref=part, dst_ref=dest, send_sem=halo_send.at[t, way], recv_sem=halo_recv.at[t, way],
            device_id=target, device_id_type=MESH,
        )

    sends = (ix < nx - 1, ix > 0, iy < ny - 1, iy > 0)
    receives = (ix > 0, ix < nx - 1, iy > 0, iy < ny - 1)
    odd = lax.rem(iy, 2) == 1
    starts = (
        (2, jnp.logical_and(sends[2], odd)), (3, sends[3]),
        (2, jnp.logical_and(sends[2], jnp.logical_not(odd))), (0, sends[0]), (1, sends[1]))

    def start_halos(t):
        for way, needed in starts:
            @pl.when(needed)
            def _():
                halo(t, way).start()

    pl.semaphore_wait(barrier, len(greeted) + ny - 1)
    start_halos(0)

    loads[0].wait()
    unpack(start_ref, write_start)
    for load in loads[1:]:
        load.wait()
    unpack(rhs_ref, write_rhs)
    for i, k in ((0, 1), (gx - 1, 2)):
        lhs[i, :, 2 * k * wide:(2 * k + 2) * wide] = jnp.zeros((rows, 2 * wide), jnp.bfloat16)
    for k, first in ((3, 0), (4, rows - rhs_count)):
        for i in range(gx):
            lhs[i, first:first + rhs_count, 2 * k * wide:(2 * k + 2) * wide] = jnp.zeros(
                (rhs_count, 2 * wide), jnp.bfloat16)
    padded[...] = jnp.zeros_like(padded)
    for first in (small - rhs_count, order + small - rhs_count):
        split_ref[first:first + rhs_count, :] = jnp.zeros((rhs_count, split_ref.shape[1]), jnp.bfloat16)
    for k in range(5):
        padded[:modes, :modes] = blocks_ref[k]
        high, low = split(padded[...])
        both = jnp.concatenate([high, low], axis=1)
        weights[2 * k * wide:(2 * k + 1) * wide, :] = both
        weights[(2 * k + 1) * wide:(2 * k + 2) * wide, :] = both

    def scale_body(i, carry):
        for k in range(5):
            for j in range(gy):
                scale[k, i, j * rhs_count:(j + 1) * rhs_count, :] = jnp.full(
                    (rhs_count, wide), coup_ref[k, i, j], jnp.float32)
        return carry
    lax.fori_loop(0, gx, scale_body, 0)

    def record(t, slot):
        for i in range(gx):
            for j in range(gy):
                e = i * gy + j
                high, low = split(field[t, i, j * rhs_count:(j + 1) * rhs_count, :])
                split_ref[slot * rhs_count:(slot + 1) * rhs_count, e * wide:(e + 1) * wide] = high
                split_ref[order + slot * rhs_count:order + (slot + 1) * rhs_count, e * wide:(e + 1) * wide] = low

    def put(k, i, lo_row, hi_row, value):
        high, low = split(value)
        lhs[i, lo_row:hi_row, 2 * k * wide:(2 * k + 1) * wide] = high
        lhs[i, lo_row:hi_row, (2 * k + 1) * wide:(2 * k + 2) * wide] = low

    def edge_dot(k, value):
        high, low = split(value)
        both = jnp.concatenate([high, low], axis=1)
        return fold(jnp.dot(both, weights[2 * k * wide:(2 * k + 2) * wide, :], preferred_element_type=jnp.float32))

    unsent = []

    def exchange(count, mine, device, buf, sems):
        def copy(d, slot):
            return pltpu.make_async_remote_copy(
                src_ref=buf.at[mine], dst_ref=buf.at[slot], send_sem=sems.at[0, d - 1], recv_sem=sems.at[1, d - 1],
                device_id=device(lax.rem(mine + d, count)), device_id_type=MESH,
            )

        def begin(value):
            buf[mine] = value
            for d in range(1, count):
                copy(d, mine).start()
            unsent.extend(copy(d, mine) for d in range(1, count))

        def end():
            for d in range(1, count):
                copy(d, lax.rem(mine + count - d, count)).wait_recv()
            total = buf[0]
            for s in range(1, count):
                total = total + buf[s]
            return total
        return begin, end

    side = lax.rem(ix, 2)

    def stages(pair, line, cross, pair_sem, line_sem, cross_sem):
        return (
            exchange(2, side, lambda s: {"ex": ix - side + s}, pair, pair_sem),
            exchange(nx // 2, ix // 2, lambda s: {"ex": 2 * s + side}, line, line_sem),
            exchange(ny, iy, lambda s: {"ey": s}, cross, cross_sem),
        )
    early_stages = stages(early_pair, early_line, early_cross, early_pair_sem, early_line_sem, early_cross_sem)
    late_stages = stages(late_pair, late_line, late_cross, late_pair_sem, late_line_sem, late_cross_sem)

    r = rhs_count
    for t in range(S + 1):
        if t > 0:
            start_halos(t)
        for i in range(gx):
            here = field[t, i]
            put(0, i, 0, rows, scale[0, i] * here)
            if i + 1 < gx:
                put(1, i + 1, 0, rows, scale[1, i + 1] * here)
            if i > 0:
                put(2, i - 1, 0, rows, scale[2, i - 1] * here)
            put(3, i, r, rows, scale[3, i, r:, :] * here[:rows - r])
            put(4, i, 0, rows - r, scale[4, i, :rows - r, :] * here[r:])
        product = fold(jnp.dot(
            lhs[...].reshape(gx * rows, 10 * wide), weights[...], preferred_element_type=jnp.float32
        )).reshape(gx, rows, wide)
        if t == 0:
            field[1] = rhs_rows[...] - product
        else:
            field[t + 1] = product
        if t > 0:
            record(t, (t - 2) % (S + 1))
        if t == S:
            early = self_products(split_ref[...], split_ref[...])
            early_stages[0][0](widen(early[:3 * r] + early[order:order + 3 * r], LANES))
            early_stages[1][0](early_stages[0][1]())
        sign = -1.0 if t == 0 else 1.0

        for way in (0, 1):
            edge = 0 if way == 0 else gx - 1

            @pl.when(receives[way])
            def _():
                halo(t, way).wait_recv()
                if t == 0:
                    for s in range(rhs_count):
                        halo_x[0, way, pl.ds(s, gy, stride=rhs_count), :] = widen(
                            raw_x[way, :, s * modes:(s + 1) * modes], wide)
                add = edge_dot(1 + way, scale[1 + way, edge] * halo_x[t, way])
                field[t + 1, edge] = field[t + 1, edge] + sign * add
        for way in (2, 3):
            first = 0 if way == 2 else rows - r

            @pl.when(receives[way])
            def _():
                halo(t, way).wait_recv()
                if t == 0:
                    for s in range(rhs_count):
                        halo_y[0, way - 2, :, s, :] = widen(raw_y[way - 2, :, s * modes:(s + 1) * modes], wide)
                value = scale[1 + way, :, first:first + r, :] * halo_y[t, way - 2]
                add = edge_dot(1 + way, value.reshape(gx * r, wide)).reshape(gx, r, wide)
                field[t + 1, :, first:first + r, :] = field[t + 1, :, first:first + r, :] + sign * add
    record(S + 1, S - 1)

    newest = jnp.concatenate([split_ref[small - r:small, :], split_ref[order + small - r:order + small, :]], axis=0)
    late = self_products(split_ref[...], newest)
    late = late[:order] + late[order:]
    late = jnp.concatenate([late[k * r:(k + 1) * r] for k in range(S + 1)], axis=1)
    late_stages[0][0](widen(late, LANES))
    late_stages[1][0](late_stages[0][1]())
    early_stages[2][0](early_stages[1][1]())
    late_stages[2][0](late_stages[1][1]())
    both, upper, zeroth = factor_early(early_stages[2][1](), r)
    both_ref[...] = both
    upper_ref[...] = upper
    zeroth_ref[...] = widen(zeroth, LANES)

    @pl.when(ix >= 0)
    def _():
        late = late_stages[2][1]()
        mixing_ref[...] = widen(
            finish_solve(both_ref[...], upper_ref[...], zeroth_ref[:, :r], late, r), LANES)
    for copy in unsent:
        copy.wait_send()

    for t in range(S + 1):
        for way in range(4):
            @pl.when(sends[way])
            def _():
                halo(t, way).wait_send()


def combine_kernel(
    dims, split_ref, mixing_ref, start_ref, field_hbm, residual_hbm,
    field_out, residual_out, rows_ref, store_sem,
):
    gx, gy, rhs_count, modes, wide = dims
    order = (S + 1) * rhs_count
    small = S * rhs_count
    turned = mixing_ref[:, :small]
    zero = jnp.zeros((rhs_count, rhs_count), jnp.float32)
    forward = jnp.concatenate([turned[:, rhs_count:small], zero, turned[:, :rhs_count]], axis=1)
    backward = jnp.concatenate([-turned[:, :small], zero], axis=1)
    mixing = jnp.concatenate([forward, backward], axis=0)
    high, low = split(mixing)
    left = jnp.concatenate([
        jnp.concatenate([high, high], axis=1), jnp.concatenate([low, low], axis=1)], axis=0)
    stores = []
    for i in range(gx):
        lo, hi = i * gy * wide, (i + 1) * gy * wide
        mixed = jnp.dot(left, split_ref[:, lo:hi], preferred_element_type=jnp.float32)
        mixed = mixed[:2 * rhs_count] + mixed[2 * rhs_count:]
        zeroth = (split_ref[order - rhs_count:order, lo:hi].astype(jnp.float32)
                  + split_ref[2 * order - rhs_count:2 * order, lo:hi].astype(jnp.float32))
        first = mixed[:rhs_count]
        second = mixed[rhs_count:] + zeroth
        for j in range(gy):
            rows_ref[0, i, j * rhs_count:(j + 1) * rhs_count, :] = first[:, j * wide:(j + 1) * wide]
            rows_ref[1, i, j * rhs_count:(j + 1) * rhs_count, :] = second[:, j * wide:(j + 1) * wide]
        for r in range(rhs_count):
            at = slice(r * modes, (r + 1) * modes)
            where = pl.ds(r, gy, stride=rhs_count)
            field_out[i, :, at] = start_ref[i, :, at] + rows_ref[0, i, where, :][:, :modes]
            residual_out[i, :, at] = rows_ref[1, i, where, :][:, :modes]
        for n, (source, dest) in enumerate(((field_out, field_hbm), (residual_out, residual_hbm))):
            stores.append(pltpu.make_async_copy(source.at[i], dest.at[i], store_sem.at[n, i]))
            stores[-1].start()
    for store in stores:
        store.wait()


def per_device(nx, ny, right_side, start_field, coupling, mode_blocks):
    gx, gy, row_width = right_side.shape
    modes = mode_blocks.shape[1]
    rhs_count = row_width // modes
    wide = -(-modes // LANES) * LANES
    dims = (gx, gy, rhs_count, modes, wide)
    rows = gy * rhs_count
    order, small = (S + 1) * rhs_count, S * rhs_count
    vmem = pl.BlockSpec(memory_space=pltpu.VMEM)
    anywhere = pl.BlockSpec(memory_space=pl.ANY)
    dma = pltpu.SemaphoreType.DMA
    f32, bf16 = jnp.float32, jnp.bfloat16
    slab = (gx, gy, row_width)
    split_shape = (2 * order, gx * gy * wide)
    early, late = ((S - 1) * rhs_count, LANES), (rhs_count, LANES)
    hbm_args = [
        pltpu.with_memory_space_constraint(x, pltpu.HBM)
        for x in (right_side, start_field, coupling, mode_blocks)]
    pieces, mixing, start_held = pl.pallas_call(
        functools.partial(basis_kernel, nx, ny, dims),
        out_shape=(jax.ShapeDtypeStruct(split_shape, bf16), jax.ShapeDtypeStruct(late, f32),
                   jax.ShapeDtypeStruct(slab, f32)),
        in_specs=[anywhere] * 4,
        out_specs=(vmem, vmem, vmem),
        scratch_shapes=[
            pltpu.VMEM(slab, f32),
            pltpu.SMEM((5, gx, gy), f32),
            pltpu.VMEM(mode_blocks.shape, f32),
            dma((4,)),
            pltpu.VMEM((S + 2, gx, rows, wide), f32),
            pltpu.VMEM((gx, rows, wide), f32),
            pltpu.VMEM((5, gx, rows, wide), f32),
            pltpu.VMEM((gx, rows, 10 * wide), bf16),
            pltpu.VMEM((10 * wide, 2 * wide), bf16),
            pltpu.VMEM((wide, wide), f32),
            pltpu.VMEM((S + 1, 2, rows, wide), f32),
            pltpu.VMEM((S + 1, 2, gx, rhs_count, wide), f32),
            pltpu.VMEM((2, gy, row_width), f32),
            pltpu.VMEM((2, gx, row_width), f32),
            *[pltpu.VMEM((count,) + shape, f32) for shape in (early, late) for count in (2, nx // 2, ny)],
            pltpu.VMEM((2 * early[0], 6 * LANES), bf16),
            pltpu.VMEM((early[0], 6 * LANES), bf16),
            pltpu.VMEM(early, f32),
            dma((S + 1, 4)),
            dma((S + 1, 4)),
            *[dma((2, max(count - 1, 1))) for _ in range(2) for count in (2, nx // 2, ny)],
        ],
        compiler_params=pltpu.CompilerParams(collective_id=0, has_side_effects=True, vmem_limit_bytes=KERNEL_VMEM),
    )(*hbm_args)
    out = jax.ShapeDtypeStruct(slab, f32)
    return pl.pallas_call(
        functools.partial(combine_kernel, dims),
        out_shape=(out, out),
        in_specs=[vmem, vmem, vmem],
        out_specs=(anywhere, anywhere),
        scratch_shapes=[
            pltpu.VMEM(slab, f32),
            pltpu.VMEM(slab, f32),
            pltpu.VMEM((2, gx, rows, wide), f32),
            dma((2, gx)),
        ],
        compiler_params=pltpu.CompilerParams(vmem_limit_bytes=KERNEL_VMEM),
    )(pieces, mixing, start_held)


def solution(mesh):
    return jax.shard_map(
        functools.partial(per_device, mesh.shape["ex"], mesh.shape["ey"]),
        mesh=mesh,
        in_specs=(P("ex", "ey", None), P("ex", "ey", None), P(None, "ex", "ey"), P()),
        out_specs=(P("ex", "ey", None), P("ex", "ey", None)),
        check_vma=False,
    )
```

```python
import functools

import jax
import jax.numpy as jnp
from jax import lax
from jax.experimental import pallas as pl
from jax.experimental.pallas import tpu as pltpu
from jax.sharding import PartitionSpec as P

S = 4
MESH = pl.DeviceIdType.MESH
LANES = 128
KERNEL_VMEM = 24 * 2**20
PANEL = 8


def split(value):
    high = value.astype(jnp.bfloat16)
    low = (value - high.astype(jnp.float32)).astype(jnp.bfloat16)
    return high, low


def fold(product):
    half = product.shape[-1] // 2
    return product[..., :half] + product[..., half:]


def widen(piece, width):
    rows, cols = piece.shape
    if cols == width:
        return piece
    return jnp.concatenate([piece, jnp.zeros((rows, width - cols), piece.dtype)], axis=1)


def self_products(left, right):
    full = lax.dot_general(left, right, (((1,), (1,)), ((), ())), preferred_element_type=jnp.float32)
    return fold(full)


def thirds(value):
    high = value.astype(jnp.bfloat16)
    rest = value - high.astype(jnp.float32)
    middle = rest.astype(jnp.bfloat16)
    return high, middle, (rest - middle.astype(jnp.float32)).astype(jnp.bfloat16)


def left_form(value):
    high, middle, low = thirds(value)
    return jnp.concatenate([high, high, middle, high, middle, low], axis=1)


def right_form(value):
    high, middle, low = thirds(value)
    return jnp.concatenate([high, middle, high, low, middle, high], axis=0)


def dot_forms(left, right):
    return jnp.dot(left, right, preferred_element_type=jnp.float32)


def at_rows(piece, first, height):
    parts = [piece, jnp.zeros((height - first - piece.shape[0], piece.shape[1]), piece.dtype)]
    if first:
        parts.insert(0, jnp.zeros((first, piece.shape[1]), piece.dtype))
    return jnp.concatenate(parts, axis=0)


def panel_lines(tile, s, first):
    lines = [jnp.broadcast_to(tile[s + q:s + q + 1, :], (8, LANES)) for q in range(PANEL)]
    pivots = [
        [jnp.broadcast_to(line[:, first + c:first + c + 1], (8, LANES)) for c in range(PANEL)] for line in lines]
    for q in range(PANEL):
        inverse = 1.0 / pivots[q][q]
        lines[q] = lines[q] * inverse
        for c in range(q + 1, PANEL):
            pivots[q][c] = pivots[q][c] * inverse
        for o in range(PANEL):
            if o != q:
                factor = pivots[o][q]
                lines[o] = lines[o] - factor * lines[q]
                for c in range(q + 1, PANEL):
                    pivots[o][c] = pivots[o][c] - factor * pivots[q][c]
    return lines


def eliminate(tile, lines, first):
    fresh = tile
    for q in range(PANEL):
        fresh = fresh - tile[:, first + q:first + q + 1] * lines[q]
    return fresh


def factor_early(early, r):
    row = lax.broadcasted_iota(jnp.int32, early.shape, 0)
    col = lax.broadcasted_iota(jnp.int32, early.shape, 1)
    matrix = jnp.where(col < 3 * r, early, (col == row + 4 * r).astype(jnp.float32))
    tiles = [matrix[8 * b:8 * b + 8, :] for b in range(3 * r // 8)]
    scaled = list(tiles)
    which = lax.broadcasted_iota(jnp.int32, (8, LANES), 0)
    for j in range(0, 3 * r, PANEL):
        b, s = divmod(j, 8)
        lines = panel_lines(tiles[b], s, j)
        for q in range(PANEL):
            scaled[b] = jnp.where(which == s + q, lines[q], scaled[b])
        if s + PANEL < 8:
            tiles[b] = jnp.where(which >= s + PANEL, eliminate(tiles[b], lines, j), tiles[b])
        for n in range(b + 1, len(tiles)):
            tiles[n] = eliminate(tiles[n], lines, j)
    lower = jnp.concatenate(tiles, axis=0)
    both = left_form(jnp.concatenate([lower, jnp.concatenate(scaled, axis=0)], axis=0))
    zeroth = dot_forms(both[3 * r:], right_form(at_rows(early[:, 4 * r:5 * r], 4 * r, LANES)))
    upper = at_rows(lower, 0, LANES).T[4 * r:7 * r]
    return both, left_form(upper), zeroth


def finish_solve(both, upper, zeroth, late, r):
    blocks = [late[:, k * r:(k + 1) * r] for k in range(5)]
    turned = dot_forms(both, right_form(at_rows(jnp.concatenate(blocks[:3], axis=0), 4 * r, LANES)))
    first = widen(at_rows(turned[:3 * r], 0, LANES), LANES).T[:r]
    right = at_rows(jnp.concatenate([turned[3 * r:], zeroth], axis=1), 0, LANES)
    rest = dot_forms(jnp.concatenate([upper, left_form(first)], axis=0), right_form(right))
    last = jnp.concatenate([blocks[3], widen(at_rows(blocks[4], 0, LANES), LANES).T[:r, :r]], axis=1)
    rest = jnp.concatenate([rest[:3 * r], last - rest[3 * r:]], axis=0)
    rest = widen(rest, LANES)
    tiles = [rest[8 * b:8 * b + 8, :] for b in range(4 * r // 8)]
    which = lax.broadcasted_iota(jnp.int32, (8, LANES), 0)
    for j in range(0, r, PANEL):
        b, s = divmod(3 * r + j, 8)
        lines = panel_lines(tiles[b], s, j)
        tiles = [eliminate(tile, lines, j) for tile in tiles]
        for q in range(PANEL):
            tiles[b] = jnp.where(which == s + q, lines[q], tiles[b])
    return jnp.concatenate(tiles, axis=0).T[r:2 * r, :]


def basis_kernel(
    nx, ny, dims,
    rhs_hbm, start_hbm, coup_hbm, blocks_hbm,
    split_ref, mixing_ref, start_ref,
    rhs_ref, coup_ref, blocks_ref, load_sem,
    field, rhs_rows, scale, lhs, weights, padded, halo_x, halo_y, raw_x, raw_y,
    early_pair, early_line, early_cross, late_pair, late_line, late_cross,
    both_ref, upper_ref, zeroth_ref, halo_send, halo_recv,
    early_pair_sem, early_line_sem, early_cross_sem, late_pair_sem, late_line_sem, late_cross_sem,
):
    gx, gy, rhs_count, modes, wide = dims
    rows = gy * rhs_count
    order = (S + 1) * rhs_count
    small = S * rhs_count
    ix, iy = lax.axis_index("ex"), lax.axis_index("ey")

    barrier = pltpu.get_barrier_semaphore()
    greeted = [d for d in range(1, nx) if d in (1, nx - 1) or d % 2 == 0]
    for d in greeted:
        pl.semaphore_signal(barrier, inc=1, device_id={"ex": lax.rem(ix + d, nx)}, device_id_type=MESH)
    for d in range(1, ny):
        pl.semaphore_signal(barrier, inc=1, device_id={"ey": lax.rem(iy + d, ny)}, device_id_type=MESH)
    loads = [
        pltpu.make_async_copy(source, dest, load_sem.at[n])
        for n, (source, dest) in enumerate((
            (start_hbm, start_ref), (rhs_hbm, rhs_ref), (coup_hbm, coup_ref), (blocks_hbm, blocks_ref)))
    ]
    for load in loads:
        load.start()

    def unpack(source, write):
        def body(i, carry):
            for r in range(rhs_count):
                piece = source[i, :, r * modes:(r + 1) * modes]
                write(i, pl.ds(r, gy, stride=rhs_count), widen(piece, wide))
            return carry
        lax.fori_loop(0, gx, body, 0)

    def write_start(i, where, value):
        field[0, i, where, :] = value

    def write_rhs(i, where, value):
        rhs_rows[i, where, :] = value

    def halo(t, way):
        target = ({"ex": lax.rem(ix + 1, nx)}, {"ex": lax.rem(ix + nx - 1, nx)},
                  {"ey": lax.rem(iy + 1, ny)}, {"ey": lax.rem(iy + ny - 1, ny)})[way]
        if t == 0:
            part = (start_hbm.at[gx - 1], start_hbm.at[0], start_hbm.at[:, gy - 1], start_hbm.at[:, 0])[way]
            dest = raw_x.at[way] if way < 2 else raw_y.at[way - 2]
        else:
            source = field.at[t]
            part = (source.at[gx - 1], source.at[0], source.at[:, rows - rhs_count:], source.at[:, :rhs_count])[way]
            dest = halo_x.at[t, way] if way < 2 else halo_y.at[t, way - 2]
        return pltpu.make_async_remote_copy(
            src_ref=part, dst_ref=dest, send_sem=halo_send.at[t, way], recv_sem=halo_recv.at[t, way],
            device_id=target, device_id_type=MESH,
        )

    sends = (ix < nx - 1, ix > 0, iy < ny - 1, iy > 0)
    receives = (ix > 0, ix < nx - 1, iy > 0, iy < ny - 1)
    odd = lax.rem(iy, 2) == 1
    starts = (
        (2, jnp.logical_and(sends[2], odd)), (3, jnp.logical_and(sends[3], jnp.logical_not(odd))),
        (0, sends[0]), (1, sends[1]),
        (2, jnp.logical_and(sends[2], jnp.logical_not(odd))), (3, jnp.logical_and(sends[3], odd)))

    def start_halos(t):
        for way, needed in starts:
            @pl.when(needed)
            def _():
                halo(t, way).start()

    pl.semaphore_wait(barrier, len(greeted) + ny - 1)
    start_halos(0)

    loads[0].wait()
    unpack(start_ref, write_start)
    for load in loads[1:]:
        load.wait()
    unpack(rhs_ref, write_rhs)
    for i, k in ((0, 1), (gx - 1, 2)):
        lhs[i, :, 2 * k * wide:(2 * k + 2) * wide] = jnp.zeros((rows, 2 * wide), jnp.bfloat16)
    for k, first in ((3, 0), (4, rows - rhs_count)):
        for i in range(gx):
            lhs[i, first:first + rhs_count, 2 * k * wide:(2 * k + 2) * wide] = jnp.zeros(
                (rhs_count, 2 * wide), jnp.bfloat16)
    padded[...] = jnp.zeros_like(padded)
    for first in (small - rhs_count, order + small - rhs_count):
        split_ref[first:first + rhs_count, :] = jnp.zeros((rhs_count, split_ref.shape[1]), jnp.bfloat16)
    for k in range(5):
        padded[:modes, :modes] = blocks_ref[k]
        high, low = split(padded[...])
        both = jnp.concatenate([high, low], axis=1)
        weights[2 * k * wide:(2 * k + 1) * wide, :] = both
        weights[(2 * k + 1) * wide:(2 * k + 2) * wide, :] = both

    def scale_body(i, carry):
        for k in range(5):
            for j in range(gy):
                scale[k, i, j * rhs_count:(j + 1) * rhs_count, :] = jnp.full(
                    (rhs_count, wide), coup_ref[k, i, j], jnp.float32)
        return carry
    lax.fori_loop(0, gx, scale_body, 0)

    def record(t, slot):
        for i in range(gx):
            for j in range(gy):
                e = i * gy + j
                high, low = split(field[t, i, j * rhs_count:(j + 1) * rhs_count, :])
                split_ref[slot * rhs_count:(slot + 1) * rhs_count, e * wide:(e + 1) * wide] = high
                split_ref[order + slot * rhs_count:order + (slot + 1) * rhs_count, e * wide:(e + 1) * wide] = low

    def put(k, i, lo_row, hi_row, value):
        high, low = split(value)
        lhs[i, lo_row:hi_row, 2 * k * wide:(2 * k + 1) * wide] = high
        lhs[i, lo_row:hi_row, (2 * k + 1) * wide:(2 * k + 2) * wide] = low

    def edge_dot(k, value):
        high, low = split(value)
        both = jnp.concatenate([high, low], axis=1)
        return fold(jnp.dot(both, weights[2 * k * wide:(2 * k + 2) * wide, :], preferred_element_type=jnp.float32))

    unsent = []

    def exchange(count, mine, device, buf, sems):
        def copy(d, slot):
            return pltpu.make_async_remote_copy(
                src_ref=buf.at[mine], dst_ref=buf.at[slot], send_sem=sems.at[0, d - 1], recv_sem=sems.at[1, d - 1],
                device_id=device(lax.rem(mine + d, count)), device_id_type=MESH,
            )

        def begin(value):
            buf[mine] = value
            for d in range(1, count):
                copy(d, mine).start()
            unsent.extend(copy(d, mine) for d in range(1, count))

        def end():
            for d in range(1, count):
                copy(d, lax.rem(mine + count - d, count)).wait_recv()
            total = buf[0]
            for s in range(1, count):
                total = total + buf[s]
            return total
        return begin, end

    side = lax.rem(ix, 2)

    def stages(pair, line, cross, pair_sem, line_sem, cross_sem):
        return (
            exchange(2, side, lambda s: {"ex": ix - side + s}, pair, pair_sem),
            exchange(nx // 2, ix // 2, lambda s: {"ex": 2 * s + side}, line, line_sem),
            exchange(ny, iy, lambda s: {"ey": s}, cross, cross_sem),
        )
    early_stages = stages(early_pair, early_line, early_cross, early_pair_sem, early_line_sem, early_cross_sem)
    late_stages = stages(late_pair, late_line, late_cross, late_pair_sem, late_line_sem, late_cross_sem)

    r = rhs_count
    for t in range(S + 1):
        if t > 0:
            start_halos(t)
        for i in range(gx):
            here = field[t, i]
            put(0, i, 0, rows, scale[0, i] * here)
            if i + 1 < gx:
                put(1, i + 1, 0, rows, scale[1, i + 1] * here)
            if i > 0:
                put(2, i - 1, 0, rows, scale[2, i - 1] * here)
            put(3, i, r, rows, scale[3, i, r:, :] * here[:rows - r])
            put(4, i, 0, rows - r, scale[4, i, :rows - r, :] * here[r:])
        product = fold(jnp.dot(
            lhs[...].reshape(gx * rows, 10 * wide), weights[...], preferred_element_type=jnp.float32
        )).reshape(gx, rows, wide)
        if t == 0:
            field[1] = rhs_rows[...] - product
        else:
            field[t + 1] = product
        if t > 0:
            record(t, (t - 2) % (S + 1))
        if t == S:
            early = self_products(split_ref[...], split_ref[...])
            early_stages[0][0](widen(early[:3 * r] + early[order:order + 3 * r], LANES))
            early_stages[1][0](early_stages[0][1]())
        sign = -1.0 if t == 0 else 1.0

        for way in (0, 1):
            edge = 0 if way == 0 else gx - 1

            @pl.when(receives[way])
            def _():
                halo(t, way).wait_recv()
                if t == 0:
                    for s in range(rhs_count):
                        halo_x[0, way, pl.ds(s, gy, stride=rhs_count), :] = widen(
                            raw_x[way, :, s * modes:(s + 1) * modes], wide)
                add = edge_dot(1 + way, scale[1 + way, edge] * halo_x[t, way])
                field[t + 1, edge] = field[t + 1, edge] + sign * add
        for way in (2, 3):
            first = 0 if way == 2 else rows - r

            @pl.when(receives[way])
            def _():
                halo(t, way).wait_recv()
                if t == 0:
                    for s in range(rhs_count):
                        halo_y[0, way - 2, :, s, :] = widen(raw_y[way - 2, :, s * modes:(s + 1) * modes], wide)
                value = scale[1 + way, :, first:first + r, :] * halo_y[t, way - 2]
                add = edge_dot(1 + way, value.reshape(gx * r, wide)).reshape(gx, r, wide)
                field[t + 1, :, first:first + r, :] = field[t + 1, :, first:first + r, :] + sign * add
    record(S + 1, S - 1)

    newest = jnp.concatenate([split_ref[small - r:small, :], split_ref[order + small - r:order + small, :]], axis=0)
    late = self_products(split_ref[...], newest)
    late = late[:order] + late[order:]
    late = jnp.concatenate([late[k * r:(k + 1) * r] for k in range(S + 1)], axis=1)
    late_stages[0][0](widen(late, LANES))
    late_stages[1][0](late_stages[0][1]())
    early_stages[2][0](early_stages[1][1]())
    late_stages[2][0](late_stages[1][1]())
    both, upper, zeroth = factor_early(early_stages[2][1](), r)
    both_ref[...] = both
    upper_ref[...] = upper
    zeroth_ref[...] = widen(zeroth, LANES)

    @pl.when(ix >= 0)
    def _():
        late = late_stages[2][1]()
        mixing_ref[...] = widen(
            finish_solve(both_ref[...], upper_ref[...], zeroth_ref[:, :r], late, r), LANES)
    for copy in unsent:
        copy.wait_send()

    for t in range(S + 1):
        for way in range(4):
            @pl.when(sends[way])
            def _():
                halo(t, way).wait_send()


def combine_kernel(
    dims, split_ref, mixing_ref, start_ref, field_hbm, residual_hbm,
    field_out, residual_out, rows_ref, store_sem,
):
    gx, gy, rhs_count, modes, wide = dims
    order = (S + 1) * rhs_count
    small = S * rhs_count
    turned = mixing_ref[:, :small]
    zero = jnp.zeros((rhs_count, rhs_count), jnp.float32)
    forward = jnp.concatenate([turned[:, rhs_count:small], zero, turned[:, :rhs_count]], axis=1)
    backward = jnp.concatenate([-turned[:, :small], zero], axis=1)
    mixing = jnp.concatenate([forward, backward], axis=0)
    high, low = split(mixing)
    left = jnp.concatenate([
        jnp.concatenate([high, high], axis=1), jnp.concatenate([low, low], axis=1)], axis=0)
    stores = []
    for i in range(gx):
        lo, hi = i * gy * wide, (i + 1) * gy * wide
        mixed = jnp.dot(left, split_ref[:, lo:hi], preferred_element_type=jnp.float32)
        mixed = mixed[:2 * rhs_count] + mixed[2 * rhs_count:]
        zeroth = (split_ref[order - rhs_count:order, lo:hi].astype(jnp.float32)
                  + split_ref[2 * order - rhs_count:2 * order, lo:hi].astype(jnp.float32))
        first = mixed[:rhs_count]
        second = mixed[rhs_count:] + zeroth
        for j in range(gy):
            rows_ref[0, i, j * rhs_count:(j + 1) * rhs_count, :] = first[:, j * wide:(j + 1) * wide]
            rows_ref[1, i, j * rhs_count:(j + 1) * rhs_count, :] = second[:, j * wide:(j + 1) * wide]
        for r in range(rhs_count):
            at = slice(r * modes, (r + 1) * modes)
            where = pl.ds(r, gy, stride=rhs_count)
            field_out[i, :, at] = start_ref[i, :, at] + rows_ref[0, i, where, :][:, :modes]
            residual_out[i, :, at] = rows_ref[1, i, where, :][:, :modes]
        for n, (source, dest) in enumerate(((field_out, field_hbm), (residual_out, residual_hbm))):
            stores.append(pltpu.make_async_copy(source.at[i], dest.at[i], store_sem.at[n, i]))
            stores[-1].start()
    for store in stores:
        store.wait()


def per_device(nx, ny, right_side, start_field, coupling, mode_blocks):
    gx, gy, row_width = right_side.shape
    modes = mode_blocks.shape[1]
    rhs_count = row_width // modes
    wide = -(-modes // LANES) * LANES
    dims = (gx, gy, rhs_count, modes, wide)
    rows = gy * rhs_count
    order, small = (S + 1) * rhs_count, S * rhs_count
    vmem = pl.BlockSpec(memory_space=pltpu.VMEM)
    anywhere = pl.BlockSpec(memory_space=pl.ANY)
    dma = pltpu.SemaphoreType.DMA
    f32, bf16 = jnp.float32, jnp.bfloat16
    slab = (gx, gy, row_width)
    split_shape = (2 * order, gx * gy * wide)
    early, late = ((S - 1) * rhs_count, LANES), (rhs_count, LANES)
    hbm_args = [
        pltpu.with_memory_space_constraint(x, pltpu.HBM)
        for x in (right_side, start_field, coupling, mode_blocks)]
    pieces, mixing, start_held = pl.pallas_call(
        functools.partial(basis_kernel, nx, ny, dims),
        out_shape=(jax.ShapeDtypeStruct(split_shape, bf16), jax.ShapeDtypeStruct(late, f32),
                   jax.ShapeDtypeStruct(slab, f32)),
        in_specs=[anywhere] * 4,
        out_specs=(vmem, vmem, vmem),
        scratch_shapes=[
            pltpu.VMEM(slab, f32),
            pltpu.SMEM((5, gx, gy), f32),
            pltpu.VMEM(mode_blocks.shape, f32),
            dma((4,)),
            pltpu.VMEM((S + 2, gx, rows, wide), f32),
            pltpu.VMEM((gx, rows, wide), f32),
            pltpu.VMEM((5, gx, rows, wide), f32),
            pltpu.VMEM((gx, rows, 10 * wide), bf16),
            pltpu.VMEM((10 * wide, 2 * wide), bf16),
            pltpu.VMEM((wide, wide), f32),
            pltpu.VMEM((S + 1, 2, rows, wide), f32),
            pltpu.VMEM((S + 1, 2, gx, rhs_count, wide), f32),
            pltpu.VMEM((2, gy, row_width), f32),
            pltpu.VMEM((2, gx, row_width), f32),
            *[pltpu.VMEM((count,) + shape, f32) for shape in (early, late) for count in (2, nx // 2, ny)],
            pltpu.VMEM((2 * early[0], 6 * LANES), bf16),
            pltpu.VMEM((early[0], 6 * LANES), bf16),
            pltpu.VMEM(early, f32),
            dma((S + 1, 4)),
            dma((S + 1, 4)),
            *[dma((2, max(count - 1, 1))) for _ in range(2) for count in (2, nx // 2, ny)],
        ],
        compiler_params=pltpu.CompilerParams(collective_id=0, has_side_effects=True, vmem_limit_bytes=KERNEL_VMEM),
    )(*hbm_args)
    out = jax.ShapeDtypeStruct(slab, f32)
    return pl.pallas_call(
        functools.partial(combine_kernel, dims),
        out_shape=(out, out),
        in_specs=[vmem, vmem, vmem],
        out_specs=(anywhere, anywhere),
        scratch_shapes=[
            pltpu.VMEM(slab, f32),
            pltpu.VMEM(slab, f32),
            pltpu.VMEM((2, gx, rows, wide), f32),
            dma((2, gx)),
        ],
        compiler_params=pltpu.CompilerParams(vmem_limit_bytes=KERNEL_VMEM),
    )(pieces, mixing, start_held)


def solution(mesh):
    return jax.shard_map(
        functools.partial(per_device, mesh.shape["ex"], mesh.shape["ey"]),
        mesh=mesh,
        in_specs=(P("ex", "ey", None), P("ex", "ey", None), P(None, "ex", "ey"), P()),
        out_specs=(P("ex", "ey", None), P("ex", "ey", None)),
        check_vma=False,
    )
```

```python
import functools

import jax
import jax.numpy as jnp
from jax import lax
from jax.experimental import pallas as pl
from jax.experimental.pallas import tpu as pltpu
from jax.sharding import PartitionSpec as P

S = 4
MESH = pl.DeviceIdType.MESH
LANES = 128
KERNEL_VMEM = 24 * 2**20
PANEL = 8


def split(value):
    high = value.astype(jnp.bfloat16)
    low = (value - high.astype(jnp.float32)).astype(jnp.bfloat16)
    return high, low


def fold(product):
    half = product.shape[-1] // 2
    return product[..., :half] + product[..., half:]


def widen(piece, width):
    rows, cols = piece.shape
    if cols == width:
        return piece
    return jnp.concatenate([piece, jnp.zeros((rows, width - cols), piece.dtype)], axis=1)


def self_products(left, right):
    full = lax.dot_general(left, right, (((1,), (1,)), ((), ())), preferred_element_type=jnp.float32)
    return fold(full)


def thirds(value):
    high = value.astype(jnp.bfloat16)
    rest = value - high.astype(jnp.float32)
    middle = rest.astype(jnp.bfloat16)
    return high, middle, (rest - middle.astype(jnp.float32)).astype(jnp.bfloat16)


def left_form(value):
    high, middle, low = thirds(value)
    return jnp.concatenate([high, high, middle, high, middle, low], axis=1)


def right_form(value):
    high, middle, low = thirds(value)
    return jnp.concatenate([high, middle, high, low, middle, high], axis=0)


def dot_forms(left, right):
    return jnp.dot(left, right, preferred_element_type=jnp.float32)


def at_rows(piece, first, height):
    parts = [piece, jnp.zeros((height - first - piece.shape[0], piece.shape[1]), piece.dtype)]
    if first:
        parts.insert(0, jnp.zeros((first, piece.shape[1]), piece.dtype))
    return jnp.concatenate(parts, axis=0)


def panel_lines(tile, s, first):
    lines = [jnp.broadcast_to(tile[s + q:s + q + 1, :], (8, LANES)) for q in range(PANEL)]
    pivots = [
        [jnp.broadcast_to(line[:, first + c:first + c + 1], (8, LANES)) for c in range(PANEL)] for line in lines]
    for q in range(PANEL):
        inverse = 1.0 / pivots[q][q]
        lines[q] = lines[q] * inverse
        for c in range(q + 1, PANEL):
            pivots[q][c] = pivots[q][c] * inverse
        for o in range(PANEL):
            if o != q:
                factor = pivots[o][q]
                lines[o] = lines[o] - factor * lines[q]
                for c in range(q + 1, PANEL):
                    pivots[o][c] = pivots[o][c] - factor * pivots[q][c]
    return lines


def eliminate(tile, lines, first):
    fresh = tile
    for q in range(PANEL):
        fresh = fresh - tile[:, first + q:first + q + 1] * lines[q]
    return fresh


def factor_early(early, r):
    row = lax.broadcasted_iota(jnp.int32, early.shape, 0)
    col = lax.broadcasted_iota(jnp.int32, early.shape, 1)
    matrix = jnp.where(col < 3 * r, early, (col == row + 4 * r).astype(jnp.float32))
    tiles = [matrix[8 * b:8 * b + 8, :] for b in range(3 * r // 8)]
    scaled = list(tiles)
    which = lax.broadcasted_iota(jnp.int32, (8, LANES), 0)
    for j in range(0, 3 * r, PANEL):
        b, s = divmod(j, 8)
        lines = panel_lines(tiles[b], s, j)
        for q in range(PANEL):
            scaled[b] = jnp.where(which == s + q, lines[q], scaled[b])
        if s + PANEL < 8:
            tiles[b] = jnp.where(which >= s + PANEL, eliminate(tiles[b], lines, j), tiles[b])
        for n in range(b + 1, len(tiles)):
            tiles[n] = eliminate(tiles[n], lines, j)
    lower = jnp.concatenate(tiles, axis=0)
    both = left_form(jnp.concatenate([lower, jnp.concatenate(scaled, axis=0)], axis=0))
    zeroth = dot_forms(both[3 * r:], right_form(at_rows(early[:, 4 * r:5 * r], 4 * r, LANES)))
    upper = at_rows(lower, 0, LANES).T[4 * r:7 * r]
    return both, left_form(upper), zeroth


def finish_solve(both, upper, zeroth, late, r):
    blocks = [late[:, k * r:(k + 1) * r] for k in range(5)]
    turned = dot_forms(both, right_form(at_rows(jnp.concatenate(blocks[:3], axis=0), 4 * r, LANES)))
    first = widen(at_rows(turned[:3 * r], 0, LANES), LANES).T[:r]
    right = at_rows(jnp.concatenate([turned[3 * r:], zeroth], axis=1), 0, LANES)
    rest = dot_forms(jnp.concatenate([upper, left_form(first)], axis=0), right_form(right))
    last = jnp.concatenate([blocks[3], widen(at_rows(blocks[4], 0, LANES), LANES).T[:r, :r]], axis=1)
    rest = jnp.concatenate([rest[:3 * r], last - rest[3 * r:]], axis=0)
    rest = widen(rest, LANES)
    tiles = [rest[8 * b:8 * b + 8, :] for b in range(4 * r // 8)]
    which = lax.broadcasted_iota(jnp.int32, (8, LANES), 0)
    for j in range(0, r, PANEL):
        b, s = divmod(3 * r + j, 8)
        lines = panel_lines(tiles[b], s, j)
        tiles = [eliminate(tile, lines, j) for tile in tiles]
        for q in range(PANEL):
            tiles[b] = jnp.where(which == s + q, lines[q], tiles[b])
    return jnp.concatenate(tiles, axis=0).T[r:2 * r, :]


def basis_kernel(
    nx, ny, dims,
    rhs_hbm, start_hbm, coup_hbm, blocks_hbm,
    split_ref, mixing_ref, start_ref,
    rhs_ref, coup_ref, blocks_ref, load_sem,
    field, rhs_rows, scale, lhs, weights, padded, halo_x, halo_y, raw_x, raw_y,
    early_pair, early_line, early_cross, late_pair, late_line, late_cross,
    both_ref, upper_ref, zeroth_ref, halo_send, halo_recv,
    early_pair_sem, early_line_sem, early_cross_sem, late_pair_sem, late_line_sem, late_cross_sem,
):
    gx, gy, rhs_count, modes, wide = dims
    rows = gy * rhs_count
    order = (S + 1) * rhs_count
    small = S * rhs_count
    ix, iy = lax.axis_index("ex"), lax.axis_index("ey")

    barrier = pltpu.get_barrier_semaphore()
    greeted = [d for d in range(1, nx) if d in (1, nx - 1) or d % 2 == 0]
    for d in greeted:
        pl.semaphore_signal(barrier, inc=1, device_id={"ex": lax.rem(ix + d, nx)}, device_id_type=MESH)
    for d in range(1, ny):
        pl.semaphore_signal(barrier, inc=1, device_id={"ey": lax.rem(iy + d, ny)}, device_id_type=MESH)
    loads = [
        pltpu.make_async_copy(source, dest, load_sem.at[n])
        for n, (source, dest) in enumerate((
            (start_hbm, start_ref), (rhs_hbm, rhs_ref), (coup_hbm, coup_ref), (blocks_hbm, blocks_ref)))
    ]
    for load in loads:
        load.start()

    def unpack(source, write):
        def body(i, carry):
            for r in range(rhs_count):
                piece = source[i, :, r * modes:(r + 1) * modes]
                write(i, pl.ds(r, gy, stride=rhs_count), widen(piece, wide))
            return carry
        lax.fori_loop(0, gx, body, 0)

    def write_start(i, where, value):
        field[0, i, where, :] = value

    def write_rhs(i, where, value):
        rhs_rows[i, where, :] = value

    def halo(t, way):
        target = ({"ex": lax.rem(ix + 1, nx)}, {"ex": lax.rem(ix + nx - 1, nx)},
                  {"ey": lax.rem(iy + 1, ny)}, {"ey": lax.rem(iy + ny - 1, ny)})[way]
        if t == 0:
            part = (start_hbm.at[gx - 1], start_hbm.at[0], start_hbm.at[:, gy - 1], start_hbm.at[:, 0])[way]
            dest = raw_x.at[way] if way < 2 else raw_y.at[way - 2]
        else:
            source = field.at[t]
            part = (source.at[gx - 1], source.at[0], source.at[:, rows - rhs_count:], source.at[:, :rhs_count])[way]
            dest = halo_x.at[t, way] if way < 2 else halo_y.at[t, way - 2]
        return pltpu.make_async_remote_copy(
            src_ref=part, dst_ref=dest, send_sem=halo_send.at[t, way], recv_sem=halo_recv.at[t, way],
            device_id=target, device_id_type=MESH,
        )

    sends = (ix < nx - 1, ix > 0, iy < ny - 1, iy > 0)
    receives = (ix > 0, ix < nx - 1, iy > 0, iy < ny - 1)
    odd = lax.rem(iy, 2) == 1
    starts = (
        (2, jnp.logical_and(sends[2], odd)), (3, jnp.logical_and(sends[3], jnp.logical_not(odd))),
        (0, sends[0]), (1, sends[1]),
        (2, jnp.logical_and(sends[2], jnp.logical_not(odd))), (3, jnp.logical_and(sends[3], odd)))

    def start_halos(t):
        for way, needed in starts:
            @pl.when(needed)
            def _():
                halo(t, way).start()

    pl.semaphore_wait(barrier, len(greeted) + ny - 1)
    start_halos(0)

    loads[0].wait()
    unpack(start_ref, write_start)
    for load in loads[1:]:
        load.wait()
    unpack(rhs_ref, write_rhs)
    for i, k in ((0, 1), (gx - 1, 2)):
        lhs[i, :, 2 * k * wide:(2 * k + 2) * wide] = jnp.zeros((rows, 2 * wide), jnp.bfloat16)
    for k, first in ((3, 0), (4, rows - rhs_count)):
        for i in range(gx):
            lhs[i, first:first + rhs_count, 2 * k * wide:(2 * k + 2) * wide] = jnp.zeros(
                (rhs_count, 2 * wide), jnp.bfloat16)
    padded[...] = jnp.zeros_like(padded)
    for first in (small - rhs_count, order + small - rhs_count):
        split_ref[first:first + rhs_count, :] = jnp.zeros((rhs_count, split_ref.shape[1]), jnp.bfloat16)
    for k in range(5):
        padded[:modes, :modes] = blocks_ref[k]
        high, low = split(padded[...])
        both = jnp.concatenate([high, low], axis=1)
        weights[2 * k * wide:(2 * k + 1) * wide, :] = both
        weights[(2 * k + 1) * wide:(2 * k + 2) * wide, :] = both

    def scale_body(i, carry):
        for k in range(5):
            for j in range(gy):
                scale[k, i, j * rhs_count:(j + 1) * rhs_count, :] = jnp.full(
                    (rhs_count, wide), coup_ref[k, i, j], jnp.float32)
        return carry
    lax.fori_loop(0, gx, scale_body, 0)

    def record(t, slot):
        for i in range(gx):
            for j in range(gy):
                e = i * gy + j
                high, low = split(field[t, i, j * rhs_count:(j + 1) * rhs_count, :])
                split_ref[slot * rhs_count:(slot + 1) * rhs_count, e * wide:(e + 1) * wide] = high
                split_ref[order + slot * rhs_count:order + (slot + 1) * rhs_count, e * wide:(e + 1) * wide] = low

    def put(k, i, lo_row, hi_row, value):
        high, low = split(value)
        lhs[i, lo_row:hi_row, 2 * k * wide:(2 * k + 1) * wide] = high
        lhs[i, lo_row:hi_row, (2 * k + 1) * wide:(2 * k + 2) * wide] = low

    def edge_dot(k, value):
        high, low = split(value)
        both = jnp.concatenate([high, low], axis=1)
        return fold(jnp.dot(both, weights[2 * k * wide:(2 * k + 2) * wide, :], preferred_element_type=jnp.float32))

    unsent = []

    def exchange(count, mine, device, buf, sems):
        def copy(d, slot):
            return pltpu.make_async_remote_copy(
                src_ref=buf.at[mine], dst_ref=buf.at[slot], send_sem=sems.at[0, d - 1], recv_sem=sems.at[1, d - 1],
                device_id=device(lax.rem(mine + d, count)), device_id_type=MESH,
            )

        def begin(value):
            buf[mine] = value
            for d in range(1, count):
                copy(d, mine).start()
            unsent.extend(copy(d, mine) for d in range(1, count))

        def end():
            for d in range(1, count):
                copy(d, lax.rem(mine + count - d, count)).wait_recv()
            total = buf[0]
            for s in range(1, count):
                total = total + buf[s]
            return total
        return begin, end

    side = lax.rem(ix, 2)

    def stages(pair, line, cross, pair_sem, line_sem, cross_sem):
        return (
            exchange(2, side, lambda s: {"ex": ix - side + s}, pair, pair_sem),
            exchange(nx // 2, ix // 2, lambda s: {"ex": 2 * s + side}, line, line_sem),
            exchange(ny, iy, lambda s: {"ey": s}, cross, cross_sem),
        )
    early_stages = stages(early_pair, early_line, early_cross, early_pair_sem, early_line_sem, early_cross_sem)
    late_stages = stages(late_pair, late_line, late_cross, late_pair_sem, late_line_sem, late_cross_sem)

    r = rhs_count
    for t in range(S + 1):
        if t > 0:
            start_halos(t)
        for i in range(gx):
            here = field[t, i]
            put(0, i, 0, rows, scale[0, i] * here)
            if i + 1 < gx:
                put(1, i + 1, 0, rows, scale[1, i + 1] * here)
            if i > 0:
                put(2, i - 1, 0, rows, scale[2, i - 1] * here)
            put(3, i, r, rows, scale[3, i, r:, :] * here[:rows - r])
            put(4, i, 0, rows - r, scale[4, i, :rows - r, :] * here[r:])
        product = fold(jnp.dot(
            lhs[...].reshape(gx * rows, 10 * wide), weights[...], preferred_element_type=jnp.float32
        )).reshape(gx, rows, wide)
        if t == 0:
            field[1] = rhs_rows[...] - product
        else:
            field[t + 1] = product
        if t > 0:
            record(t, (t - 2) % (S + 1))
        if t == S:
            early = self_products(split_ref[...], split_ref[...])
            early_stages[0][0](widen(early[:3 * r] + early[order:order + 3 * r], LANES))
            early_stages[1][0](early_stages[0][1]())
        sign = -1.0 if t == 0 else 1.0

        for way, needed in ((0, jnp.logical_and(receives[0], side == 1)), (1, receives[1]),
                            (0, jnp.logical_and(receives[0], side == 0))):
            edge = 0 if way == 0 else gx - 1

            @pl.when(needed)
            def _():
                halo(t, way).wait_recv()
                if t == 0:
                    for s in range(rhs_count):
                        halo_x[0, way, pl.ds(s, gy, stride=rhs_count), :] = widen(
                            raw_x[way, :, s * modes:(s + 1) * modes], wide)
                add = edge_dot(1 + way, scale[1 + way, edge] * halo_x[t, way])
                field[t + 1, edge] = field[t + 1, edge] + sign * add
        for way in (2, 3):
            first = 0 if way == 2 else rows - r

            @pl.when(receives[way])
            def _():
                halo(t, way).wait_recv()
                if t == 0:
                    for s in range(rhs_count):
                        halo_y[0, way - 2, :, s, :] = widen(raw_y[way - 2, :, s * modes:(s + 1) * modes], wide)
                value = scale[1 + way, :, first:first + r, :] * halo_y[t, way - 2]
                add = edge_dot(1 + way, value.reshape(gx * r, wide)).reshape(gx, r, wide)
                field[t + 1, :, first:first + r, :] = field[t + 1, :, first:first + r, :] + sign * add
    record(S + 1, S - 1)

    newest = jnp.concatenate([split_ref[small - r:small, :], split_ref[order + small - r:order + small, :]], axis=0)
    late = self_products(split_ref[...], newest)
    late = late[:order] + late[order:]
    late = jnp.concatenate([late[k * r:(k + 1) * r] for k in range(S + 1)], axis=1)
    late_stages[0][0](widen(late, LANES))
    late_stages[1][0](late_stages[0][1]())
    early_stages[2][0](early_stages[1][1]())
    late_stages[2][0](late_stages[1][1]())
    both, upper, zeroth = factor_early(early_stages[2][1](), r)
    both_ref[...] = both
    upper_ref[...] = upper
    zeroth_ref[...] = widen(zeroth, LANES)

    @pl.when(ix >= 0)
    def _():
        late = late_stages[2][1]()
        mixing_ref[...] = widen(
            finish_solve(both_ref[...], upper_ref[...], zeroth_ref[:, :r], late, r), LANES)
    for copy in unsent:
        copy.wait_send()

    for t in range(S + 1):
        for way in range(4):
            @pl.when(sends[way])
            def _():
                halo(t, way).wait_send()


def combine_kernel(
    dims, split_ref, mixing_ref, start_ref, field_hbm, residual_hbm,
    field_out, residual_out, rows_ref, store_sem,
):
    gx, gy, rhs_count, modes, wide = dims
    order = (S + 1) * rhs_count
    small = S * rhs_count
    turned = mixing_ref[:, :small]
    zero = jnp.zeros((rhs_count, rhs_count), jnp.float32)
    forward = jnp.concatenate([turned[:, rhs_count:small], zero, turned[:, :rhs_count]], axis=1)
    backward = jnp.concatenate([-turned[:, :small], zero], axis=1)
    mixing = jnp.concatenate([forward, backward], axis=0)
    high, low = split(mixing)
    left = jnp.concatenate([
        jnp.concatenate([high, high], axis=1), jnp.concatenate([low, low], axis=1)], axis=0)
    stores = []
    for i in range(gx):
        lo, hi = i * gy * wide, (i + 1) * gy * wide
        mixed = jnp.dot(left, split_ref[:, lo:hi], preferred_element_type=jnp.float32)
        mixed = mixed[:2 * rhs_count] + mixed[2 * rhs_count:]
        zeroth = (split_ref[order - rhs_count:order, lo:hi].astype(jnp.float32)
                  + split_ref[2 * order - rhs_count:2 * order, lo:hi].astype(jnp.float32))
        first = mixed[:rhs_count]
        second = mixed[rhs_count:] + zeroth
        for j in range(gy):
            rows_ref[0, i, j * rhs_count:(j + 1) * rhs_count, :] = first[:, j * wide:(j + 1) * wide]
            rows_ref[1, i, j * rhs_count:(j + 1) * rhs_count, :] = second[:, j * wide:(j + 1) * wide]
        for r in range(rhs_count):
            at = slice(r * modes, (r + 1) * modes)
            where = pl.ds(r, gy, stride=rhs_count)
            field_out[i, :, at] = start_ref[i, :, at] + rows_ref[0, i, where, :][:, :modes]
            residual_out[i, :, at] = rows_ref[1, i, where, :][:, :modes]
        for n, (source, dest) in enumerate(((field_out, field_hbm), (residual_out, residual_hbm))):
            stores.append(pltpu.make_async_copy(source.at[i], dest.at[i], store_sem.at[n, i]))
            stores[-1].start()
    for store in stores:
        store.wait()


def per_device(nx, ny, right_side, start_field, coupling, mode_blocks):
    gx, gy, row_width = right_side.shape
    modes = mode_blocks.shape[1]
    rhs_count = row_width // modes
    wide = -(-modes // LANES) * LANES
    dims = (gx, gy, rhs_count, modes, wide)
    rows = gy * rhs_count
    order, small = (S + 1) * rhs_count, S * rhs_count
    vmem = pl.BlockSpec(memory_space=pltpu.VMEM)
    anywhere = pl.BlockSpec(memory_space=pl.ANY)
    dma = pltpu.SemaphoreType.DMA
    f32, bf16 = jnp.float32, jnp.bfloat16
    slab = (gx, gy, row_width)
    split_shape = (2 * order, gx * gy * wide)
    early, late = ((S - 1) * rhs_count, LANES), (rhs_count, LANES)
    hbm_args = [
        pltpu.with_memory_space_constraint(x, pltpu.HBM)
        for x in (right_side, start_field, coupling, mode_blocks)]
    pieces, mixing, start_held = pl.pallas_call(
        functools.partial(basis_kernel, nx, ny, dims),
        out_shape=(jax.ShapeDtypeStruct(split_shape, bf16), jax.ShapeDtypeStruct(late, f32),
                   jax.ShapeDtypeStruct(slab, f32)),
        in_specs=[anywhere] * 4,
        out_specs=(vmem, vmem, vmem),
        scratch_shapes=[
            pltpu.VMEM(slab, f32),
            pltpu.SMEM((5, gx, gy), f32),
            pltpu.VMEM(mode_blocks.shape, f32),
            dma((4,)),
            pltpu.VMEM((S + 2, gx, rows, wide), f32),
            pltpu.VMEM((gx, rows, wide), f32),
            pltpu.VMEM((5, gx, rows, wide), f32),
            pltpu.VMEM((gx, rows, 10 * wide), bf16),
            pltpu.VMEM((10 * wide, 2 * wide), bf16),
            pltpu.VMEM((wide, wide), f32),
            pltpu.VMEM((S + 1, 2, rows, wide), f32),
            pltpu.VMEM((S + 1, 2, gx, rhs_count, wide), f32),
            pltpu.VMEM((2, gy, row_width), f32),
            pltpu.VMEM((2, gx, row_width), f32),
            *[pltpu.VMEM((count,) + shape, f32) for shape in (early, late) for count in (2, nx // 2, ny)],
            pltpu.VMEM((2 * early[0], 6 * LANES), bf16),
            pltpu.VMEM((early[0], 6 * LANES), bf16),
            pltpu.VMEM(early, f32),
            dma((S + 1, 4)),
            dma((S + 1, 4)),
            *[dma((2, max(count - 1, 1))) for _ in range(2) for count in (2, nx // 2, ny)],
        ],
        compiler_params=pltpu.CompilerParams(collective_id=0, has_side_effects=True, vmem_limit_bytes=KERNEL_VMEM),
    )(*hbm_args)
    out = jax.ShapeDtypeStruct(slab, f32)
    return pl.pallas_call(
        functools.partial(combine_kernel, dims),
        out_shape=(out, out),
        in_specs=[vmem, vmem, vmem],
        out_specs=(anywhere, anywhere),
        scratch_shapes=[
            pltpu.VMEM(slab, f32),
            pltpu.VMEM(slab, f32),
            pltpu.VMEM((2, gx, rows, wide), f32),
            dma((2, gx)),
        ],
        compiler_params=pltpu.CompilerParams(vmem_limit_bytes=KERNEL_VMEM),
    )(pieces, mixing, start_held)


def solution(mesh):
    return jax.shard_map(
        functools.partial(per_device, mesh.shape["ex"], mesh.shape["ey"]),
        mesh=mesh,
        in_specs=(P("ex", "ey", None), P("ex", "ey", None), P(None, "ex", "ey"), P()),
        out_specs=(P("ex", "ey", None), P("ex", "ey", None)),
        check_vma=False,
    )
```
